1024 devices in a mesh: section: 32 (over y, z_lo), ctx: 4 (over z_hi, core), dp: 8 (over x).
Axes of the slice: x: 8, y: 8, z: 8 (z_hi: 2, z_lo: 4; z = z_hi * 4 + z_lo), core: 2. Of those that a mesh axis runs over, the one named last changes fastest.
Arguments:
- q_in: bfloat16 [8, 32, 512, 2048], P('dp', 'section', 'ctx'), may hold values from -6 to 6
- key_input: bfloat16 [8, 32, 512, 512], P('dp', 'section', 'ctx'), may hold values from -6 to 6
- value_input: bfloat16 [8, 32, 512, 512], P('dp', 'section', 'ctx'), may hold values from -6 to 6
- output_saved: bfloat16 [8, 32, 512, 2048], P('dp', 'section', 'ctx'), may hold values from -6 to 6
- output_gradient: bfloat16 [8, 32, 512, 2048], P('dp', 'section', 'ctx'), may hold values from -6 to 6
- lse: float32 [8, 32, 16, 512], P('dp', 'section', None, 'ctx'), may hold values from 2 to 5
- bias_q: bfloat16 [32, 2048], P('section'), may hold values from -3 to 3
- key_bias: bfloat16 [32, 512], P('section'), may hold values from -3 to 3
- value_bias: bfloat16 [32, 512], P('section'), may hold values from -3 to 3
Outputs:
- recv_q: bfloat16 [8, 32, 512, 2048], P('dp', 'section', 'ctx')
- recv_k: bfloat16 [8, 32, 512, 512], P('dp', 'section', 'ctx')
- recv_v: bfloat16 [8, 32, 512, 512], P('dp', 'section', 'ctx')
- grad_bq: float32 [32, 2048], P('section')
- grad_bk: float32 [32, 512], P('section')
- grad_bv: float32 [32, 512], P('section')
The draws below stay inside these ranges and needn't reach their ends.
All inputs are finite; a program needn't handle non-finite values.
Results may differ from the reference program's by a relative error of at most 0.0035.
The reference program's roundings to bfloat16 on the way count: a program that leaves them out, or rounds other values in their place, can miss the bound.
Values may be sent and summed in bfloat16 or wider, within the bound.
No kernel may reach another device: no remote copies, remote signals or barrier semaphores. Data moves between devices by JAX's collectives and lax.ppermute only.
A program may use at most 32 MiB of HBM per device.

```python
import math
import jax
import jax.numpy as jnp
from jax import lax

QUERY_HEADS = 16
KEY_VALUE_HEADS = 4
HEAD_SIZE = 128
TOK_DEV = 128
BATCH_TOKENS = 512
RELAY_SECTIONS = 32
DATA_REPLICAS = 8
N_SECTION = 32
N_CTX = 4
N_DP = 8


def shard_levels(own_key, shape, split, least, largest):
    level = 1.0
    for dim, blocks in split:
        heights = jax.random.uniform(jax.random.fold_in(jax.random.fold_in(own_key, 6), dim), (blocks,), jnp.float32, least / len(split), largest / len(split))
        level = level * jnp.repeat(jnp.exp(heights), shape[dim] // blocks).reshape((-1,) + (1,) * (len(shape) - 1 - dim))
    return level


def scatter_about(own_key, extent, deviation, bound, split=(), kind=jnp.bfloat16):
    values = deviation * jax.random.normal(own_key, extent, jnp.float32)
    if split:
        values = values * shard_levels(own_key, extent, split, -0.22, 0.18)
    return jnp.clip(values, -bound, bound).astype(kind)


def setup_inputs(seed: int = 0) -> dict:
    splits = jax.random.split(jax.random.key(seed), 10)
    return {
        "q_in": scatter_about(splits[0], (DATA_REPLICAS, RELAY_SECTIONS, BATCH_TOKENS, QUERY_HEADS * HEAD_SIZE), 1.0, 6.0, ((0, 8), (1, 32), (2, 4))),
        "key_input": scatter_about(splits[1], (DATA_REPLICAS, RELAY_SECTIONS, BATCH_TOKENS, KEY_VALUE_HEADS * HEAD_SIZE), 1.0, 6.0, ((0, 8), (1, 32), (2, 4))),
        "value_input": scatter_about(splits[2], (DATA_REPLICAS, RELAY_SECTIONS, BATCH_TOKENS, KEY_VALUE_HEADS * HEAD_SIZE), 1.0, 6.0, ((0, 8), (1, 32), (2, 4))),
        "output_saved": scatter_about(splits[3], (DATA_REPLICAS, RELAY_SECTIONS, BATCH_TOKENS, QUERY_HEADS * HEAD_SIZE), 1.0, 6.0, ((0, 8), (1, 32), (2, 4))),
        "output_gradient": scatter_about(splits[4], (DATA_REPLICAS, RELAY_SECTIONS, BATCH_TOKENS, QUERY_HEADS * HEAD_SIZE), 1.0, 6.0, ((0, 8), (1, 32), (2, 4))),
        "lse": jnp.clip(2.0 + 3.0 * jax.random.uniform(splits[5], (DATA_REPLICAS, RELAY_SECTIONS, QUERY_HEADS, BATCH_TOKENS), jnp.float32) ** shard_levels(splits[5], (DATA_REPLICAS, RELAY_SECTIONS, QUERY_HEADS, BATCH_TOKENS), ((0, 8), (1, 32), (3, 4)), -0.2, 0.2), 2.0, 5.0),
        "bias_q": scatter_about(splits[6], (RELAY_SECTIONS, QUERY_HEADS * HEAD_SIZE), 0.5, 3.0, ((0, 32),)),
        "key_bias": scatter_about(splits[7], (RELAY_SECTIONS, KEY_VALUE_HEADS * HEAD_SIZE), 0.5, 3.0, ((0, 32),)),
        "value_bias": scatter_about(splits[8], (RELAY_SECTIONS, KEY_VALUE_HEADS * HEAD_SIZE), 0.5, 3.0, ((0, 32),)),
    }


def token_position(rows, block_rows, block_count):
    half_rows = block_rows // 2
    owner = rows // block_rows
    local = rows % block_rows
    early = owner * half_rows + local
    late = (2 * block_count - 1 - owner) * half_rows + local - half_rows
    return jnp.where(local < half_rows, early, late).astype(jnp.int32)

def backward_item(operands):
    q_in, key_input, value_input, output_saved, output_gradient, lse, bias_q, key_bias, value_bias = operands
    token_rows = q_in.shape[0]
    query_groups = QUERY_HEADS // KEY_VALUE_HEADS
    att_scale = 1.0 / math.sqrt(HEAD_SIZE)
    query_lowered = (q_in.astype(jnp.float32) + bias_q.astype(jnp.float32)).astype(jnp.bfloat16)
    key_lowered = (key_input.astype(jnp.float32) + key_bias.astype(jnp.float32)).astype(jnp.bfloat16)
    value_lowered = (value_input.astype(jnp.float32) + value_bias.astype(jnp.float32)).astype(jnp.bfloat16)
    query_grouped = query_lowered.astype(jnp.float32).reshape(token_rows, KEY_VALUE_HEADS, query_groups, HEAD_SIZE)
    key_row_list = key_lowered.astype(jnp.float32).reshape(token_rows, KEY_VALUE_HEADS, HEAD_SIZE)
    value_row_list = value_lowered.astype(jnp.float32).reshape(token_rows, KEY_VALUE_HEADS, HEAD_SIZE)
    output_gradient_grouped = output_gradient.astype(jnp.float32).reshape(token_rows, KEY_VALUE_HEADS, query_groups, HEAD_SIZE)
    output_grouped = output_saved.astype(jnp.float32).reshape(token_rows, KEY_VALUE_HEADS, query_groups, HEAD_SIZE)
    row_delta = jnp.transpose(lax.optimization_barrier(jnp.sum(output_gradient_grouped * output_grouped, axis=-1)), (1, 2, 0))
    scores = jnp.einsum('ikgd,jkd->kgij', query_grouped, key_row_list) * att_scale
    positions = token_position(jnp.arange(token_rows, dtype=jnp.int32), TOK_DEV, N_CTX)
    causal = positions[None, :] <= positions[:, None]
    logsumexp_grouped = lse.reshape(KEY_VALUE_HEADS, query_groups, token_rows)
    soft_prob = jnp.where(causal, jnp.exp(scores - logsumexp_grouped[..., None]), 0.0)
    grad_prob = jnp.einsum('ikgd,jkd->kgij', output_gradient_grouped, value_row_list)
    grad_score = soft_prob * (grad_prob - row_delta[..., None])
    prob_low = lax.optimization_barrier(soft_prob.astype(jnp.bfloat16)).astype(jnp.float32)
    score_low = lax.optimization_barrier(grad_score.astype(jnp.bfloat16)).astype(jnp.float32)
    grad_q = jnp.einsum('kgij,jkd->ikgd', score_low, key_row_list) * att_scale
    key_gradient = jnp.einsum('kgij,ikgd->jkd', score_low, query_grouped) * att_scale
    value_gradient = jnp.einsum('kgij,ikgd->jkd', prob_low, output_gradient_grouped)
    grad_q = grad_q.reshape(token_rows, QUERY_HEADS * HEAD_SIZE)
    key_gradient = key_gradient.reshape(token_rows, KEY_VALUE_HEADS * HEAD_SIZE)
    value_gradient = value_gradient.reshape(token_rows, KEY_VALUE_HEADS * HEAD_SIZE)
    return (grad_q.astype(jnp.bfloat16), key_gradient.astype(jnp.bfloat16), value_gradient.astype(jnp.bfloat16), lax.optimization_barrier(jnp.sum(grad_q, axis=0)), lax.optimization_barrier(jnp.sum(key_gradient, axis=0)), lax.optimization_barrier(jnp.sum(value_gradient, axis=0)))

def reference(q_in, key_input, value_input, output_saved, output_gradient, lse, bias_q, key_bias, value_bias):
    entries = N_DP * N_SECTION

    def flatten_items(array):
        return array.reshape((entries,) + array.shape[2:])

    def section_bias(bias):
        return jnp.broadcast_to(bias[None], (N_DP,) + bias.shape).reshape((entries, bias.shape[1]))
    results = lax.map(backward_item, (flatten_items(q_in), flatten_items(key_input), flatten_items(value_input), flatten_items(output_saved), flatten_items(output_gradient), flatten_items(lse), section_bias(bias_q), section_bias(key_bias), section_bias(value_bias)))
    grad_q, key_gradient, value_gradient, sum_q, sum_k, sum_v = results

    def unflatten(array):
        return array.reshape((N_DP, N_SECTION) + array.shape[1:])

    def passed_back(array):
        whole = unflatten(array)
        return jnp.concatenate([whole[:, 1:], jnp.zeros_like(whole[:, :1])], axis=1)
    return (passed_back(grad_q), passed_back(key_gradient), passed_back(value_gradient), lax.optimization_barrier(jnp.sum(unflatten(sum_q), axis=0)), lax.optimization_barrier(jnp.sum(unflatten(sum_k), axis=0)), lax.optimization_barrier(jnp.sum(unflatten(sum_v), axis=0)))
```

```python
import functools
import math

import jax
import jax.numpy as jnp
from jax import lax
from jax.experimental import pallas as pl
from jax.experimental.pallas import tpu as pltpu
from jax.sharding import PartitionSpec as P

HEAD_SIZE = 128
ROWS = 128
HALF = ROWS // 2
Q_HEADS = 16
KV_HEADS = 4
Q_OWN = Q_HEADS // 2
KV_OWN = KV_HEADS // 2
GROUP = Q_HEADS // KV_HEADS
SCALE = 1.0 / math.sqrt(HEAD_SIZE)
LOG2E = math.log2(math.e)
AT_Q = 0
AT_G = AT_Q + Q_OWN
AT_K = AT_G + Q_OWN
AT_V = AT_K + KV_OWN
AT_ROW = AT_V + KV_OWN
PACK = AT_ROW + 1
BF16 = jnp.bfloat16
F32 = jnp.float32
LOW = -1e30

SMEM = pl.BlockSpec(memory_space=pltpu.SMEM)
VMEM = pl.BlockSpec(memory_space=pltpu.VMEM)


def call(kernel, outs, n_in, name, flops=0, moved=0, scratch=()):
    return pl.pallas_call(
        kernel,
        out_shape=outs,
        in_specs=[SMEM] + [VMEM] * n_in,
        out_specs=[VMEM] * len(outs),
        scratch_shapes=list(scratch),
        name=name,
        cost_estimate=pl.CostEstimate(flops=flops, bytes_accessed=moved, transcendentals=0),
    )


def shape(*dims, dtype=BF16):
    return jax.ShapeDtypeStruct(dims, dtype)


def split3(x):
    a = x.astype(BF16)
    rest = x - a.astype(F32)
    b = rest.astype(BF16)
    return a, b, (rest - b.astype(F32)).astype(BF16)


def prep_kernel(at, q, k, v, o, g, lse, bq, bk, bv, own, send, kv1s, kv1x, kv2s, kv2x):
    core = at[0] % 2
    for pack, side in ((own, core), (send, 1 - core)):
        base = pl.multiple_of(side * (Q_OWN * HEAD_SIZE), Q_OWN * HEAD_SIZE)
        kv_base = pl.multiple_of(side * (KV_OWN * HEAD_SIZE), KV_OWN * HEAD_SIZE)
        deltas = []
        for h in range(Q_OWN):
            cols = pl.ds(base + h * HEAD_SIZE, HEAD_SIZE)
            pack[AT_Q + h] = (q[:, cols].astype(F32) + bq[:, cols].astype(F32)).astype(BF16)
            grad = g[:, cols]
            pack[AT_G + h] = grad
            deltas.append(
                jnp.sum(grad.astype(F32) * o[:, cols].astype(F32), axis=1, keepdims=True)
            )
        for h in range(KV_OWN):
            cols = pl.ds(kv_base + h * HEAD_SIZE, HEAD_SIZE)
            kb = (k[:, cols].astype(F32) + bk[:, cols].astype(F32)).astype(BF16)
            vb = (v[:, cols].astype(F32) + bv[:, cols].astype(F32)).astype(BF16)
            pack[AT_K + h] = kb
            pack[AT_V + h] = vb
            first, second = (kv1s, kv2s) if pack is own else (kv1x, kv2x)
            first[h] = kb[:HALF]
            second[h] = kb[HALF:]
            first[KV_OWN + h] = vb[:HALF]
            second[KV_OWN + h] = vb[HALF:]
        delta = jnp.concatenate(deltas + [jnp.zeros((ROWS, HEAD_SIZE - Q_OWN), F32)], axis=1).T
        heads = pl.ds(pl.multiple_of(side * Q_OWN, Q_OWN), Q_OWN)
        stats = jnp.concatenate(
            [p.astype(F32) for p in split3(lse[heads, :])]
            + [p.astype(F32) for p in split3(delta[:Q_OWN])]
            + [jnp.zeros((ROWS - 6 * Q_OWN, HEAD_SIZE), F32)],
            axis=0,
        )
        pack[AT_ROW] = stats.astype(BF16)


def row_stats(own, recv):
    def one(pack):
        s = pack[AT_ROW].astype(F32)
        n = Q_OWN
        lse = (s[:n] + s[n : 2 * n]) + s[2 * n : 3 * n]
        delta = (s[3 * n : 4 * n] + s[4 * n : 5 * n]) + s[5 * n : 6 * n]
        return lse * LOG2E, delta

    (la, da), (lb, db) = one(own), one(recv)
    return jnp.concatenate([la, lb], axis=1), jnp.concatenate([da, db], axis=1)


def positions(index, dim, ctx_count, alternate):
    i = lax.broadcasted_iota(jnp.int32, (2 * ROWS, 2 * ROWS), dim)
    part = i // HALF
    late = part // 2 if alternate else part % 2
    other = part % 2 if alternate else part // 2
    block = jnp.where(other == 1, index + 1 - 2 * (index % 2), index)
    half = jnp.where(late == 1, 2 * ctx_count - 1 - block, block)
    return half * HALF + i % HALF


def head_terms(q, g, k, v, bias, lse, delta):
    s = lax.dot_general(k, q, (((1,), (1,)), ((), ())), preferred_element_type=F32)
    dp = lax.dot_general(v, g, (((1,), (1,)), ((), ())), preferred_element_type=F32)
    p = jnp.exp2(s * (SCALE * LOG2E) + (bias - lse))
    ds = (p * (dp - delta)).astype(BF16)
    p = p.astype(BF16)
    gv = jnp.dot(p, g, preferred_element_type=F32)
    gk = jnp.dot(ds, q, preferred_element_type=F32)
    gq = lax.dot_general(ds, k, (((0,), (0,)), ((), ())), preferred_element_type=F32)
    return gq, gk, gv


def local_kernel(at, own, recv, gq_out, gkv_out, *, ctx_count):
    kpos = positions(at[0], 0, ctx_count, False)
    qpos = positions(at[0], 1, ctx_count, False)
    bias = jnp.where(kpos <= qpos, 0.0, LOW)
    lse, delta = row_stats(own, recv)
    for kv in range(KV_OWN):
        k = jnp.concatenate([own[AT_K + kv], recv[AT_K + kv]], axis=0)
        v = jnp.concatenate([own[AT_V + kv], recv[AT_V + kv]], axis=0)
        gk = gv = None
        for j in range(GROUP):
            h = kv * GROUP + j
            q = jnp.concatenate([own[AT_Q + h], recv[AT_Q + h]], axis=0)
            g = jnp.concatenate([own[AT_G + h], recv[AT_G + h]], axis=0)
            tq, tk, tv = head_terms(q, g, k, v, bias, lse[h : h + 1], delta[h : h + 1])
            gq_out[h] = tq
            gk = tk if gk is None else gk + tk
            gv = tv if gv is None else gv + tv
        gkv_out[kv] = gk * SCALE
        gkv_out[KV_OWN + kv] = gv


def remote_kernel(
    at, own, recv, kv1s, kv1x, kv2s, kv2x, gq_in, gkv_in, gq_same, gq_other, gr1, gr2, sums, *, ctx_count
):
    far = (at[0] + ctx_count // 2) % ctx_count
    kpos = positions(far, 0, ctx_count, True)
    qpos = positions(at[0], 1, ctx_count, False)
    bias = jnp.where(kpos <= qpos, 0.0, LOW)
    lse, delta = row_stats(own, recv)
    for kv in range(KV_OWN):
        k = jnp.concatenate([r[kv] for r in (kv1s, kv1x, kv2s, kv2x)], axis=0)
        v = jnp.concatenate([r[KV_OWN + kv] for r in (kv1s, kv1x, kv2s, kv2x)], axis=0)
        gk = gv = None
        for j in range(GROUP):
            h = kv * GROUP + j
            q = jnp.concatenate([own[AT_Q + h], recv[AT_Q + h]], axis=0)
            g = jnp.concatenate([own[AT_G + h], recv[AT_G + h]], axis=0)
            tq, tk, tv = head_terms(q, g, k, v, bias, lse[h : h + 1], delta[h : h + 1])
            gq = (gq_in[h] + tq) * SCALE
            gq_same[h] = gq[:ROWS].astype(BF16)
            gq_other[h] = gq[ROWS:].astype(BF16)
            sums[h : h + 1, :] = jnp.sum(gq, axis=0, keepdims=True)
            gk = tk if gk is None else gk + tk
            gv = tv if gv is None else gv + tv
        for at_row, t in ((kv, gk * SCALE), (KV_OWN + kv, gv)):
            gr1[at_row] = t[:ROWS]
            gr2[at_row] = t[ROWS:]
            total = jnp.sum(t, axis=0, keepdims=True) + jnp.sum(
                gkv_in[at_row], axis=0, keepdims=True
            )
            sums[Q_OWN + at_row : Q_OWN + at_row + 1, :] = total


def kv_kernel(at, gkv, r1, r2, same, other):
    for i in range(2 * KV_OWN):
        same[i, :HALF] = (gkv[i, :HALF] + r1[i, :HALF]).astype(BF16)
        same[i, HALF:] = (gkv[i, HALF:ROWS] + r2[i, :HALF]).astype(BF16)
        other[i, :HALF] = (gkv[i, ROWS : ROWS + HALF] + r1[i, HALF:]).astype(BF16)
        other[i, HALF:] = (gkv[i, ROWS + HALF :] + r2[i, HALF:]).astype(BF16)


def join_q_kernel(at, same, other, out):
    core = at[0] % 2
    for part, side in ((same, core), (other, 1 - core)):
        base = pl.multiple_of(side * (Q_OWN * HEAD_SIZE), Q_OWN * HEAD_SIZE)
        for h in range(Q_OWN):
            out[:, pl.ds(base + h * HEAD_SIZE, HEAD_SIZE)] = part[h]


def join_kv_kernel(at, same, other, out_k, out_v):
    core = at[0] % 2
    for part, side in ((same, core), (other, 1 - core)):
        base = pl.multiple_of(side * (KV_OWN * HEAD_SIZE), KV_OWN * HEAD_SIZE)
        for h in range(KV_OWN):
            cols = pl.ds(base + h * HEAD_SIZE, HEAD_SIZE)
            out_k[:, cols] = part[h]
            out_v[:, cols] = part[KV_OWN + h]


def join_sums_kernel(at, same, other, out_q, out_k, out_v):
    core = at[0] % 2
    for part, side in ((same, core), (other, 1 - core)):
        base = pl.multiple_of(side * (Q_OWN * HEAD_SIZE), Q_OWN * HEAD_SIZE)
        kv_base = pl.multiple_of(side * (KV_OWN * HEAD_SIZE), KV_OWN * HEAD_SIZE)
        for h in range(Q_OWN):
            out_q[:, pl.ds(base + h * HEAD_SIZE, HEAD_SIZE)] = part[h : h + 1, :]
        for h in range(KV_OWN):
            cols = pl.ds(kv_base + h * HEAD_SIZE, HEAD_SIZE)
            out_k[:, cols] = part[Q_OWN + h : Q_OWN + h + 1, :]
            out_v[:, cols] = part[Q_OWN + KV_OWN + h : Q_OWN + KV_OWN + h + 1, :]


def swapped(value, axis, bit):
    size = lax.axis_size(axis)
    return lax.ppermute(value, axis, [(i, i ^ bit) for i in range(size)])


def body(q_in, k_in, v_in, o_in, g_in, lse, bq, bk, bv):
    n = lax.axis_size("ctx")
    at = lax.axis_index("ctx").astype(jnp.int32).reshape(1)
    chips = n // 2
    blocks = lambda count, rows=ROWS, dtype=BF16: shape(count, rows, HEAD_SIZE, dtype=dtype)

    own, send, kv1s, kv1x, kv2s, kv2x = call(
        prep_kernel,
        [blocks(PACK), blocks(PACK)] + [blocks(2 * KV_OWN, HALF)] * 4,
        9,
        "prep",
        moved=4 << 20,
    )(at, q_in[0, 0], k_in[0, 0], v_in[0, 0], o_in[0, 0], g_in[0, 0], lse[0, 0], bq, bk, bv)

    up = lambda x, bit: lax.ppermute(x, "ctx", [(i, (i ^ bit) % chips) for i in range(chips, n)])
    down = lambda x: lax.ppermute(x, "ctx", [(i, i + chips) for i in range(chips)])
    kv1s, kv1x = swapped(kv1s, "ctx", chips), swapped(kv1x, "ctx", chips + 1)
    kv2s, kv2x = up(kv2s, 0), up(kv2x, 1)
    recv = swapped(send, "ctx", 1)

    gq, gkv = call(
        functools.partial(local_kernel, ctx_count=n),
        [blocks(Q_OWN, 2 * ROWS, F32), blocks(2 * KV_OWN, 2 * ROWS, F32)],
        2,
        "local",
        flops=700_000_000,
        moved=3 << 20,
    )(at, own, recv)
    gq_same, gq_other, gr1, gr2, sums = call(
        functools.partial(remote_kernel, ctx_count=n),
        [blocks(Q_OWN)] * 2 + [blocks(2 * KV_OWN, ROWS, F32)] * 2 + [shape(Q_OWN + 2 * KV_OWN, HEAD_SIZE, dtype=F32)],
        8,
        "remote",
        flops=700_000_000,
        moved=4 << 20,
    )(at, own, recv, kv1s, kv1x, kv2s, kv2x, gq, gkv)

    r1, r2 = swapped(gr1, "ctx", chips), down(gr2)

    def before(x, bit):
        count = lax.axis_size("section") * n
        pairs = []
        for s in range(1, lax.axis_size("section")):
            pairs += [(s * n + c, (s - 1) * n + (c ^ bit)) for c in range(n)]
        return lax.ppermute(x, ("section", "ctx"), pairs)

    gq_same, gq_other = before(gq_same, 0), before(gq_other, 1)
    kv_same, kv_other = call(kv_kernel, [blocks(2 * KV_OWN)] * 2, 3, "kv", moved=2 << 20)(
        at, gkv, r1, r2
    )
    kv_same, kv_other = before(kv_same, 0), before(kv_other, 1)

    sums = sums + swapped(sums, "ctx", chips)
    step = 1
    while step < lax.axis_size("dp"):
        sums = sums + swapped(sums, "dp", step)
        step *= 2
    sums_other = swapped(sums, "ctx", 1)
    sum_q, sum_k, sum_v = call(
        join_sums_kernel,
        [
            shape(1, Q_HEADS * HEAD_SIZE, dtype=F32),
            shape(1, KV_HEADS * HEAD_SIZE, dtype=F32),
            shape(1, KV_HEADS * HEAD_SIZE, dtype=F32),
        ],
        2,
        "join_sums",
    )(at, sums, sums_other)
    (recv_q,) = call(join_q_kernel, [shape(ROWS, Q_HEADS * HEAD_SIZE)], 2, "join_q", moved=1 << 20)(
        at, gq_same, gq_other
    )
    recv_k, recv_v = call(
        join_kv_kernel, [shape(ROWS, KV_HEADS * HEAD_SIZE)] * 2, 2, "join_kv", moved=1 << 19
    )(at, kv_same, kv_other)
    return (recv_q[None, None], recv_k[None, None], recv_v[None, None], sum_q, sum_k, sum_v)


def solution(mesh):
    return jax.shard_map(
        body,
        mesh=mesh,
        in_specs=(
            P("dp", "section", "ctx", None),
            P("dp", "section", "ctx", None),
            P("dp", "section", "ctx", None),
            P("dp", "section", "ctx", None),
            P("dp", "section", "ctx", None),
            P("dp", "section", None, "ctx"),
            P("section", None),
            P("section", None),
            P("section", None),
        ),
        out_specs=(
            P("dp", "section", "ctx", None),
            P("dp", "section", "ctx", None),
            P("dp", "section", "ctx", None),
            P("section", None),
            P("section", None),
            P("section", None),
        ),
        check_vma=False,
    )
```

```python
import functools
import math

import jax
import jax.numpy as jnp
from jax import lax
from jax.experimental import pallas as pl
from jax.experimental.pallas import tpu as pltpu
from jax.sharding import PartitionSpec as P


HEAD_SIZE = 128
ROWS = 128
HALF = ROWS // 2
Q_HEADS = 16
KV_HEADS = 4
Q_OWN = Q_HEADS // 2
KV_OWN = KV_HEADS // 2
GROUP = Q_HEADS // KV_HEADS
SCALE = 1.0 / math.sqrt(HEAD_SIZE)
LOG2E = math.log2(math.e)
AT_Q = 0
AT_G = AT_Q + Q_OWN
AT_K = AT_G + Q_OWN
AT_V = AT_K + KV_OWN
AT_ROW = AT_V + KV_OWN
PACK = AT_ROW + 1
SUM_ROWS = 16
BF16 = jnp.bfloat16
F32 = jnp.float32
LOW = -1e30
KERNEL_VMEM = 24 << 20

SMEM = pl.BlockSpec(memory_space=pltpu.SMEM)
VMEM = pl.BlockSpec(memory_space=pltpu.VMEM)


def call(kernel, outs, n_in, flops=0, moved=0, keep=True, vmem=KERNEL_VMEM):
    keep = len(outs) if keep is True else int(keep)
    outs = [pltpu.VMEM(o.shape, o.dtype) for o in outs[:keep]] + outs[keep:]
    run = pl.pallas_call(
        kernel,
        out_shape=outs,
        in_specs=[SMEM] + [VMEM] * n_in,
        out_specs=[VMEM] * len(outs),
        compiler_params=pltpu.CompilerParams(vmem_limit_bytes=vmem),
        cost_estimate=pl.CostEstimate(flops=flops, bytes_accessed=moved, transcendentals=0),
    )
    return run


def held(x):
    return pltpu.with_memory_space_constraint(x, pltpu.VMEM)


def shape(*dims, dtype=BF16):
    return jax.ShapeDtypeStruct(dims, dtype)


def split3(x):
    a = x.astype(BF16)
    rest = x - a.astype(F32)
    b = rest.astype(BF16)
    return a, b, (rest - b.astype(F32)).astype(BF16)


def prep_kernel(at, q, k, v, o, g, lse, bq, bk, bv, own, send, kv1, kv2):
    core = at[0] % 2
    for pack, side in ((own, core), (send, 1 - core)):
        base = pl.multiple_of(side * (Q_OWN * HEAD_SIZE), Q_OWN * HEAD_SIZE)
        kv_base = pl.multiple_of(side * (KV_OWN * HEAD_SIZE), KV_OWN * HEAD_SIZE)
        deltas = []
        for h in range(Q_OWN):
            cols = pl.ds(base + h * HEAD_SIZE, HEAD_SIZE)
            pack[AT_Q + h] = (q[:, cols].astype(F32) + bq[:, cols].astype(F32)).astype(BF16)
            grad = g[:, cols]
            pack[AT_G + h] = grad
            deltas.append(
                jnp.sum(grad.astype(F32) * o[:, cols].astype(F32), axis=1, keepdims=True)
            )
        for h in range(KV_OWN):
            cols = pl.ds(kv_base + h * HEAD_SIZE, HEAD_SIZE)
            kb = (k[:, cols].astype(F32) + bk[:, cols].astype(F32)).astype(BF16)
            vb = (v[:, cols].astype(F32) + bv[:, cols].astype(F32)).astype(BF16)
            pack[AT_K + h] = kb
            pack[AT_V + h] = vb
            to = 0 if pack is own else 1
            kv1[to, h] = kb[:HALF]
            kv2[to, h] = kb[HALF:]
            kv1[to, KV_OWN + h] = vb[:HALF]
            kv2[to, KV_OWN + h] = vb[HALF:]
        delta = jnp.concatenate(deltas + [jnp.zeros((ROWS, HEAD_SIZE - Q_OWN), F32)], axis=1).T
        heads = pl.ds(pl.multiple_of(side * Q_OWN, Q_OWN), Q_OWN)
        stats = jnp.concatenate(
            [p.astype(F32) for p in split3(lse[heads, :])]
            + [p.astype(F32) for p in split3(delta[:Q_OWN])]
            + [jnp.zeros((ROWS - 6 * Q_OWN, HEAD_SIZE), F32)],
            axis=0,
        )
        pack[AT_ROW] = stats.astype(BF16)


def row_stats(own, recv):
    def one(pack):
        s = pack[AT_ROW].astype(F32)
        n = Q_OWN
        lse = (s[:n] + s[n : 2 * n]) + s[2 * n : 3 * n]
        delta = (s[3 * n : 4 * n] + s[4 * n : 5 * n]) + s[5 * n : 6 * n]
        return lse * LOG2E, delta

    (la, da), (lb, db) = one(own), one(recv)
    return jnp.concatenate([la, lb], axis=1), jnp.concatenate([da, db], axis=1)


def positions(index, dim, ctx_count, alternate):
    i = lax.broadcasted_iota(jnp.int32, (2 * ROWS, 2 * ROWS), dim)
    part = i // HALF
    late = part // 2 if alternate else part % 2
    other = part % 2 if alternate else part // 2
    block = jnp.where(other == 1, index + 1 - 2 * (index % 2), index)
    half = jnp.where(late == 1, 2 * ctx_count - 1 - block, block)
    return half * HALF + i % HALF


def head_terms(q, g, k, v, bias, lse, delta):
    s = lax.dot_general(k, q, (((1,), (1,)), ((), ())), preferred_element_type=F32)
    dp = lax.dot_general(v, g, (((1,), (1,)), ((), ())), preferred_element_type=F32)
    p = jnp.exp2(s * (SCALE * LOG2E) + (bias - lse))
    ds = (p * (dp - delta)).astype(BF16)
    p = p.astype(BF16)
    gv = jnp.dot(p, g, preferred_element_type=F32)
    gk = jnp.dot(ds, q, preferred_element_type=F32)
    gq = lax.dot_general(ds, k, (((0,), (0,)), ((), ())), preferred_element_type=F32)
    return gq, gk, gv


def local_kernel(at, own, recv, gq_out, gkv_out, *, ctx_count):
    kpos = positions(at[0], 0, ctx_count, False)
    qpos = positions(at[0], 1, ctx_count, False)
    bias = jnp.where(kpos <= qpos, 0.0, LOW)
    lse, delta = row_stats(own, recv)
    for kv in range(KV_OWN):
        k = jnp.concatenate([own[AT_K + kv], recv[AT_K + kv]], axis=0)
        v = jnp.concatenate([own[AT_V + kv], recv[AT_V + kv]], axis=0)
        gk = gv = None
        for j in range(GROUP):
            h = kv * GROUP + j
            q = jnp.concatenate([own[AT_Q + h], recv[AT_Q + h]], axis=0)
            g = jnp.concatenate([own[AT_G + h], recv[AT_G + h]], axis=0)
            tq, tk, tv = head_terms(q, g, k, v, bias, lse[h : h + 1], delta[h : h + 1])
            gq_out[h] = tq
            gk = tk if gk is None else gk + tk
            gv = tv if gv is None else gv + tv
        gkv_out[kv] = gk * SCALE
        gkv_out[KV_OWN + kv] = gv


def remote_kernel(
    at, own, recv, kv1, kv2, cross, gq_in, gkv_in, gq_same, gq_other, gr1, gr2, sums, *, ctx_count
):
    far_kv = (kv1.at[0], cross.at[0], kv2.at[0], cross.at[1])
    totals = []
    far = (at[0] + ctx_count // 2) % ctx_count
    kpos = positions(far, 0, ctx_count, True)
    qpos = positions(at[0], 1, ctx_count, False)
    bias = jnp.where(kpos <= qpos, 0.0, LOW)
    lse, delta = row_stats(own, recv)
    for kv in range(KV_OWN):
        k = jnp.concatenate([r[kv] for r in far_kv], axis=0)
        v = jnp.concatenate([r[KV_OWN + kv] for r in far_kv], axis=0)
        gk = gv = None
        for j in range(GROUP):
            h = kv * GROUP + j
            q = jnp.concatenate([own[AT_Q + h], recv[AT_Q + h]], axis=0)
            g = jnp.concatenate([own[AT_G + h], recv[AT_G + h]], axis=0)
            tq, tk, tv = head_terms(q, g, k, v, bias, lse[h : h + 1], delta[h : h + 1])
            gq = (gq_in[h] + tq) * SCALE
            gq_same[h] = gq[:ROWS].astype(BF16)
            gq_other[h] = gq[ROWS:].astype(BF16)
            totals.append((h, jnp.sum(gq, axis=0, keepdims=True)))
            gk = tk if gk is None else gk + tk
            gv = tv if gv is None else gv + tv
        for at_row, t in ((kv, gk * SCALE), (KV_OWN + kv, gv)):
            gr1[at_row] = t[:ROWS]
            gr2[at_row] = t[ROWS:]
            total = jnp.sum(t, axis=0, keepdims=True) + jnp.sum(
                gkv_in[at_row], axis=0, keepdims=True
            )
            totals.append((Q_OWN + at_row, total))
    pad = SUM_ROWS - len(totals)
    totals = [t for _, t in sorted(totals, key=lambda t: t[0])] + [jnp.zeros((pad, HEAD_SIZE), F32)]
    sums[...] = jnp.broadcast_to(jnp.concatenate(totals, axis=0)[None], sums.shape)


def cross_kernel(at, kv1, kv2, out):
    out[0] = kv1[1]
    out[1] = kv2[1]


def kv_kernel(at, gkv, r1, r2, same, other):
    for i in range(2 * KV_OWN):
        same[i, :HALF] = (gkv[i, :HALF] + r1[i, :HALF]).astype(BF16)
        same[i, HALF:] = (gkv[i, HALF:ROWS] + r2[i, :HALF]).astype(BF16)
        other[i, :HALF] = (gkv[i, ROWS : ROWS + HALF] + r1[i, HALF:]).astype(BF16)
        other[i, HALF:] = (gkv[i, ROWS + HALF :] + r2[i, HALF:]).astype(BF16)


def join_q_kernel(at, same, other, out):
    core = at[0] % 2
    for part, side in ((same, core), (other, 1 - core)):
        base = pl.multiple_of(side * (Q_OWN * HEAD_SIZE), Q_OWN * HEAD_SIZE)
        for h in range(Q_OWN):
            out[:, pl.ds(base + h * HEAD_SIZE, HEAD_SIZE)] = part[h]


def join_kv_kernel(at, same, other, out_k, out_v):
    core = at[0] % 2
    for part, side in ((same, core), (other, 1 - core)):
        base = pl.multiple_of(side * (KV_OWN * HEAD_SIZE), KV_OWN * HEAD_SIZE)
        for h in range(KV_OWN):
            cols = pl.ds(base + h * HEAD_SIZE, HEAD_SIZE)
            out_k[:, cols] = part[h]
            out_v[:, cols] = part[KV_OWN + h]


def join_sums_kernel(at, parts, out_q, out_k, out_v):
    ctx_count, dp_count = parts.shape[:2]
    for core in range(2):
        total = None
        for c in range(core, ctx_count, 2):
            for r in range(dp_count):
                total = parts[c, r] if total is None else total + parts[c, r]
        for h in range(Q_OWN):
            at_col = (core * Q_OWN + h) * HEAD_SIZE
            out_q[:, at_col : at_col + HEAD_SIZE] = total[h : h + 1]
        for h in range(KV_OWN):
            at_col = (core * KV_OWN + h) * HEAD_SIZE
            row = Q_OWN + h
            out_k[:, at_col : at_col + HEAD_SIZE] = total[row : row + 1]
            row += KV_OWN
            out_v[:, at_col : at_col + HEAD_SIZE] = total[row : row + 1]


def swapped(value, axis, bit):
    size = lax.axis_size(axis)
    return lax.ppermute(value, axis, [(i, i ^ bit) for i in range(size)])


def body(q_in, k_in, v_in, o_in, g_in, lse, bq, bk, bv):
    n = lax.axis_size("ctx")
    at = lax.axis_index("ctx").astype(jnp.int32).reshape(1)
    chips = n // 2
    blocks = lambda count, rows=ROWS, dtype=BF16: shape(count, rows, HEAD_SIZE, dtype=dtype)

    dp = lax.axis_size("dp")
    own, send, kv1, kv2 = call(
        prep_kernel,
        [blocks(PACK), blocks(PACK)] + [shape(2, 2 * KV_OWN, HALF, HEAD_SIZE)] * 2,
        9,
        moved=4 << 20,
        keep=2,
        vmem=60 << 20,
    )(at, q_in[0, 0], k_in[0, 0], v_in[0, 0], o_in[0, 0], g_in[0, 0], lse[0, 0], bq, bk, bv)

    up = [(i + chips, i) for i in range(chips)]
    down = [(i, i + chips) for i in range(chips)]
    kv1 = held(swapped(kv1, "ctx", chips))
    kv2 = held(lax.ppermute(kv2, "ctx", up))
    recv = held(swapped(send, "ctx", 1))
    own = held(own)

    gq, gkv = call(
        functools.partial(local_kernel, ctx_count=n),
        [blocks(Q_OWN, 2 * ROWS, F32), blocks(2 * KV_OWN, 2 * ROWS, F32)],
        2,
        flops=700_000_000,
        moved=3 << 20,
    )(at, own, recv)
    gq, gkv = held(gq), held(gkv)
    (cross,) = call(cross_kernel, [shape(2, 2 * KV_OWN, HALF, HEAD_SIZE)], 2)(at, kv1, kv2)
    cross = held(swapped(cross, "ctx", 1))
    gq_same, gq_other, gr1, gr2, sums = call(
        functools.partial(remote_kernel, ctx_count=n),
        [blocks(Q_OWN)] * 2
        + [blocks(2 * KV_OWN, ROWS, F32)] * 2
        + [shape(n * dp, SUM_ROWS, HEAD_SIZE, dtype=F32)],
        7,
        flops=700_000_000,
        moved=4 << 20,
        keep=4,
    )(at, own, recv, kv1, kv2, cross, gq, gkv)

    r1 = held(swapped(gr1, "ctx", chips))
    r2 = held(lax.ppermute(gr2, "ctx", down))

    def before(x, bit):
        pairs = []
        for s in range(1, lax.axis_size("section")):
            pairs += [(s * n + c, (s - 1) * n + (c ^ bit)) for c in range(n)]
        return held(lax.ppermute(x, ("section", "ctx"), pairs))

    gq_same, gq_other = before(gq_same, 0), before(gq_other, 1)
    sums = lax.all_to_all(sums, ("ctx", "dp"), 0, 0, tiled=True)
    sum_q, sum_k, sum_v = call(
        join_sums_kernel,
        [
            shape(1, Q_HEADS * HEAD_SIZE, dtype=F32),
            shape(1, KV_HEADS * HEAD_SIZE, dtype=F32),
            shape(1, KV_HEADS * HEAD_SIZE, dtype=F32),
        ],
        1,
        keep=False,
    )(at, held(sums.reshape(n, dp, SUM_ROWS, HEAD_SIZE)))
    kv_same, kv_other = call(kv_kernel, [blocks(2 * KV_OWN)] * 2, 3, moved=2 << 20)(at, gkv, r1, r2)
    kv_same, kv_other = before(kv_same, 0), before(kv_other, 1)
    (recv_q,) = call(
        join_q_kernel, [shape(ROWS, Q_HEADS * HEAD_SIZE)], 2, moved=1 << 20, keep=False
    )(at, gq_same, gq_other)
    recv_k, recv_v = call(
        join_kv_kernel, [shape(ROWS, KV_HEADS * HEAD_SIZE)] * 2, 2, moved=1 << 19, keep=False
    )(at, kv_same, kv_other)
    return (recv_q[None, None], recv_k[None, None], recv_v[None, None], sum_q, sum_k, sum_v)


def solution(mesh):
    return jax.shard_map(
        body,
        mesh=mesh,
        in_specs=(
            P("dp", "section", "ctx", None),
            P("dp", "section", "ctx", None),
            P("dp", "section", "ctx", None),
            P("dp", "section", "ctx", None),
            P("dp", "section", "ctx", None),
            P("dp", "section", None, "ctx"),
            P("section", None),
            P("section", None),
            P("section", None),
        ),
        out_specs=(
            P("dp", "section", "ctx", None),
            P("dp", "section", "ctx", None),
            P("dp", "section", "ctx", None),
            P("section", None),
            P("section", None),
            P("section", None),
        ),
        check_vma=False,
    )
```

```python
import functools
import math

import jax
import jax.numpy as jnp
from jax import lax
from jax.experimental import pallas as pl
from jax.experimental.pallas import tpu as pltpu
from jax.sharding import PartitionSpec as P


HEAD_SIZE = 128
ROWS = 128
HALF = ROWS // 2
Q_HEADS = 16
KV_HEADS = 4
Q_OWN = Q_HEADS // 2
KV_OWN = KV_HEADS // 2
GROUP = Q_HEADS // KV_HEADS
SCALE = 1.0 / math.sqrt(HEAD_SIZE)
LOG2E = math.log2(math.e)
AT_Q = 0
AT_G = AT_Q + Q_OWN
AT_K = AT_G + Q_OWN
AT_V = AT_K + KV_OWN
AT_ROW = AT_V + KV_OWN
PACK = AT_ROW + 1
SUM_ROWS = 16
BF16 = jnp.bfloat16
F32 = jnp.float32
LOW = -1e30
KERNEL_VMEM = 24 << 20

SMEM = pl.BlockSpec(memory_space=pltpu.SMEM)
VMEM = pl.BlockSpec(memory_space=pltpu.VMEM)


def call(kernel, outs, n_in, flops=0, moved=0, keep=True, vmem=KERNEL_VMEM):
    keep = len(outs) if keep is True else int(keep)
    outs = [pltpu.VMEM(o.shape, o.dtype) for o in outs[:keep]] + outs[keep:]
    run = pl.pallas_call(
        kernel,
        out_shape=outs,
        in_specs=[SMEM] + [VMEM] * n_in,
        out_specs=[VMEM] * len(outs),
        compiler_params=pltpu.CompilerParams(vmem_limit_bytes=vmem),
        cost_estimate=pl.CostEstimate(flops=flops, bytes_accessed=moved, transcendentals=0),
    )
    return run


def held(x):
    return pltpu.with_memory_space_constraint(x, pltpu.VMEM)


def shape(*dims, dtype=BF16):
    return jax.ShapeDtypeStruct(dims, dtype)


def split3(x):
    a = x.astype(BF16)
    rest = x - a.astype(F32)
    b = rest.astype(BF16)
    return a, b, (rest - b.astype(F32)).astype(BF16)


def prep_kernel(at, q, k, v, o, g, lse, bq, bk, bv, own, send, kvz):
    core = at[0] % 2
    for pack, side in ((own, core), (send, 1 - core)):
        base = pl.multiple_of(side * (Q_OWN * HEAD_SIZE), Q_OWN * HEAD_SIZE)
        kv_base = pl.multiple_of(side * (KV_OWN * HEAD_SIZE), KV_OWN * HEAD_SIZE)
        deltas = []
        for h in range(Q_OWN):
            cols = pl.ds(base + h * HEAD_SIZE, HEAD_SIZE)
            pack[AT_Q + h] = (q[:, cols].astype(F32) + bq[:, cols].astype(F32)).astype(BF16)
            grad = g[:, cols]
            pack[AT_G + h] = grad
            deltas.append(
                jnp.sum(grad.astype(F32) * o[:, cols].astype(F32), axis=1, keepdims=True)
            )
        for h in range(KV_OWN):
            cols = pl.ds(kv_base + h * HEAD_SIZE, HEAD_SIZE)
            kb = (k[:, cols].astype(F32) + bk[:, cols].astype(F32)).astype(BF16)
            vb = (v[:, cols].astype(F32) + bv[:, cols].astype(F32)).astype(BF16)
            pack[AT_K + h] = kb
            pack[AT_V + h] = vb
            to = 0 if pack is own else 1
            for late in range(2):
                rows = slice(late * HALF, (late + 1) * HALF)
                kvz[to, late, h] = kb[rows]
                kvz[to, late, KV_OWN + h] = vb[rows]
        delta = jnp.concatenate(deltas + [jnp.zeros((ROWS, HEAD_SIZE - Q_OWN), F32)], axis=1).T
        heads = pl.ds(pl.multiple_of(side * Q_OWN, Q_OWN), Q_OWN)
        stats = jnp.concatenate(
            [p.astype(F32) for p in split3(lse[heads, :])]
            + [p.astype(F32) for p in split3(delta[:Q_OWN])]
            + [jnp.zeros((ROWS - 6 * Q_OWN, HEAD_SIZE), F32)],
            axis=0,
        )
        pack[AT_ROW] = stats.astype(BF16)


def row_stats(own, recv):
    def one(pack):
        s = pack[AT_ROW].astype(F32)
        n = Q_OWN
        lse = (s[:n] + s[n : 2 * n]) + s[2 * n : 3 * n]
        delta = (s[3 * n : 4 * n] + s[4 * n : 5 * n]) + s[5 * n : 6 * n]
        return lse * LOG2E, delta

    (la, da), (lb, db) = one(own), one(recv)
    return jnp.concatenate([la, lb], axis=1), jnp.concatenate([da, db], axis=1)


def positions(index, dim, ctx_count, alternate):
    i = lax.broadcasted_iota(jnp.int32, (2 * ROWS, 2 * ROWS), dim)
    part = i // HALF
    late = part // 2 if alternate else part % 2
    other = part % 2 if alternate else part // 2
    block = jnp.where(other == 1, index + 1 - 2 * (index % 2), index)
    half = jnp.where(late == 1, 2 * ctx_count - 1 - block, block)
    return half * HALF + i % HALF


def head_terms(q, g, k, v, bias, lse, delta):
    s = lax.dot_general(k, q, (((1,), (1,)), ((), ())), preferred_element_type=F32)
    dp = lax.dot_general(v, g, (((1,), (1,)), ((), ())), preferred_element_type=F32)
    p = jnp.exp2(s * (SCALE * LOG2E) + (bias - lse))
    ds = (p * (dp - delta)).astype(BF16)
    p = p.astype(BF16)
    gv = jnp.dot(p, g, preferred_element_type=F32)
    gk = jnp.dot(ds, q, preferred_element_type=F32)
    gq = lax.dot_general(ds, k, (((0,), (0,)), ((), ())), preferred_element_type=F32)
    return gq, gk, gv


def local_kernel(at, own, recv, gq_out, same, other, kv_sums, *, ctx_count):
    kpos = positions(at[0], 0, ctx_count, False)
    qpos = positions(at[0], 1, ctx_count, False)
    bias = jnp.where(kpos <= qpos, 0.0, LOW)
    lse, delta = row_stats(own, recv)
    for kv in range(KV_OWN):
        k = jnp.concatenate([own[AT_K + kv], recv[AT_K + kv]], axis=0)
        v = jnp.concatenate([own[AT_V + kv], recv[AT_V + kv]], axis=0)
        gk = gv = None
        for j in range(GROUP):
            h = kv * GROUP + j
            q = jnp.concatenate([own[AT_Q + h], recv[AT_Q + h]], axis=0)
            g = jnp.concatenate([own[AT_G + h], recv[AT_G + h]], axis=0)
            tq, tk, tv = head_terms(q, g, k, v, bias, lse[h : h + 1], delta[h : h + 1])
            gq_out[h] = tq
            gk = tk if gk is None else gk + tk
            gv = tv if gv is None else gv + tv
        for row, t in ((kv, gk * SCALE), (KV_OWN + kv, gv)):
            same[row] = t[:ROWS]
            other[row] = t[ROWS:]
            kv_sums[row : row + 1, :] = jnp.sum(t, axis=0, keepdims=True)


def remote_kernel(
    at, own, recv, far, cross, gq_in, kv_sums, gq_same, gq_other, r1s, r1x, r2s, r2x, sums, *, ctx_count
):
    far_kv = (far.at[0, 0], cross.at[0], far.at[0, 1], cross.at[1])
    totals = []
    far_index = (at[0] + ctx_count // 2) % ctx_count
    kpos = positions(far_index, 0, ctx_count, True)
    qpos = positions(at[0], 1, ctx_count, False)
    bias = jnp.where(kpos <= qpos, 0.0, LOW)
    lse, delta = row_stats(own, recv)
    for kv in range(KV_OWN):
        k = jnp.concatenate([r[kv] for r in far_kv], axis=0)
        v = jnp.concatenate([r[KV_OWN + kv] for r in far_kv], axis=0)
        gk = gv = None
        for j in range(GROUP):
            h = kv * GROUP + j
            q = jnp.concatenate([own[AT_Q + h], recv[AT_Q + h]], axis=0)
            g = jnp.concatenate([own[AT_G + h], recv[AT_G + h]], axis=0)
            tq, tk, tv = head_terms(q, g, k, v, bias, lse[h : h + 1], delta[h : h + 1])
            gq = (gq_in[h] + tq) * SCALE
            gq_same[h] = gq[:ROWS].astype(BF16)
            gq_other[h] = gq[ROWS:].astype(BF16)
            totals.append((h, jnp.sum(gq, axis=0, keepdims=True)))
            gk = tk if gk is None else gk + tk
            gv = tv if gv is None else gv + tv
        for row, t in ((kv, gk * SCALE), (KV_OWN + kv, gv)):
            for part, out in enumerate((r1s, r1x, r2s, r2x)):
                out[row] = t[part * HALF : (part + 1) * HALF]
            total = jnp.sum(t, axis=0, keepdims=True) + kv_sums[row : row + 1, :]
            totals.append((Q_OWN + row, total))
    pad = SUM_ROWS - len(totals)
    totals = [t for _, t in sorted(totals, key=lambda t: t[0])] + [jnp.zeros((pad, HEAD_SIZE), F32)]
    sums[...] = jnp.broadcast_to(jnp.concatenate(totals, axis=0)[None], sums.shape)


def cross_kernel(at, far, out):
    out[...] = far[1]


def join_q_kernel(at, same, other, out):
    core = at[0] % 2
    for part, side in ((same, core), (other, 1 - core)):
        base = pl.multiple_of(side * (Q_OWN * HEAD_SIZE), Q_OWN * HEAD_SIZE)
        for h in range(Q_OWN):
            out[:, pl.ds(base + h * HEAD_SIZE, HEAD_SIZE)] = part[h]


def join_kv_kernel(at, same, other, r1s, r1x, r2s, r2x, out_k, out_v):
    core = at[0] % 2
    for near, first, second, side in ((same, r1s, r2s, core), (other, r1x, r2x, 1 - core)):
        base = pl.multiple_of(side * (KV_OWN * HEAD_SIZE), KV_OWN * HEAD_SIZE)
        for h in range(KV_OWN):
            cols = pl.ds(base + h * HEAD_SIZE, HEAD_SIZE)
            for out, i in ((out_k, h), (out_v, KV_OWN + h)):
                out[:HALF, cols] = (near[i, :HALF] + first[i]).astype(BF16)
                out[HALF:, cols] = (near[i, HALF:] + second[i]).astype(BF16)


def join_sums_kernel(at, parts, out_q, out_k, out_v):
    ctx_count, dp_count = parts.shape[:2]
    for core in range(2):
        total = None
        for c in range(core, ctx_count, 2):
            for r in range(dp_count):
                total = parts[c, r] if total is None else total + parts[c, r]
        for h in range(Q_OWN):
            at_col = (core * Q_OWN + h) * HEAD_SIZE
            out_q[:, at_col : at_col + HEAD_SIZE] = total[h : h + 1]
        for h in range(KV_OWN):
            at_col = (core * KV_OWN + h) * HEAD_SIZE
            row = Q_OWN + h
            out_k[:, at_col : at_col + HEAD_SIZE] = total[row : row + 1]
            row += KV_OWN
            out_v[:, at_col : at_col + HEAD_SIZE] = total[row : row + 1]


def swapped(value, axis, bit):
    size = lax.axis_size(axis)
    return lax.ppermute(value, axis, [(i, i ^ bit) for i in range(size)])


def body(q_in, k_in, v_in, o_in, g_in, lse, bq, bk, bv):
    n = lax.axis_size("ctx")
    at = lax.axis_index("ctx").astype(jnp.int32).reshape(1)
    chips = n // 2
    blocks = lambda count, rows=ROWS, dtype=BF16: shape(count, rows, HEAD_SIZE, dtype=dtype)

    dp = lax.axis_size("dp")
    own, send, kvz = call(
        prep_kernel,
        [blocks(PACK), blocks(PACK), shape(2, 2, 2 * KV_OWN, HALF, HEAD_SIZE)],
        9,
        moved=4 << 20,
        vmem=60 << 20,
    )(at, q_in[0, 0], k_in[0, 0], v_in[0, 0], o_in[0, 0], g_in[0, 0], lse[0, 0], bq, bk, bv)

    far = held(swapped(kvz, "ctx", chips))
    recv = held(swapped(send, "ctx", 1))
    own = held(own)

    gq, kv_same, kv_other, kv_sums = call(
        functools.partial(local_kernel, ctx_count=n),
        [blocks(Q_OWN, 2 * ROWS, F32)]
        + [blocks(2 * KV_OWN, ROWS, F32)] * 2
        + [shape(2 * KV_OWN, HEAD_SIZE, dtype=F32)],
        2,
        flops=700_000_000,
        moved=3 << 20,
    )(at, own, recv)

    def before(x, bit, senders=range(n)):
        pairs = []
        for s in range(1, lax.axis_size("section")):
            pairs += [(s * n + c, (s - 1) * n + (c ^ bit)) for c in senders]
        return held(lax.ppermute(x, ("section", "ctx"), pairs))

    kv_same, kv_other = before(kv_same, 0), before(kv_other, 1)
    (cross,) = call(cross_kernel, [shape(2, 2 * KV_OWN, HALF, HEAD_SIZE)], 1)(at, far)
    cross = held(swapped(cross, "ctx", 1))
    gq_same, gq_other, r1s, r1x, r2s, r2x, sums = call(
        functools.partial(remote_kernel, ctx_count=n),
        [blocks(Q_OWN)] * 2
        + [blocks(2 * KV_OWN, HALF, F32)] * 4
        + [shape(n * dp, SUM_ROWS, HEAD_SIZE, dtype=F32)],
        6,
        flops=700_000_000,
        moved=4 << 20,
        keep=6,
    )(at, own, recv, far, cross, held(gq), held(kv_sums))

    r2s = before(r2s, chips, range(chips))
    r2x = before(r2x, chips + 1, range(chips))
    r1s, r1x = before(r1s, chips), before(r1x, chips + 1)
    gq_same, gq_other = before(gq_same, 0), before(gq_other, 1)
    sums = lax.all_to_all(sums, ("ctx", "dp"), 0, 0, tiled=True)
    sum_q, sum_k, sum_v = call(
        join_sums_kernel,
        [
            shape(1, Q_HEADS * HEAD_SIZE, dtype=F32),
            shape(1, KV_HEADS * HEAD_SIZE, dtype=F32),
            shape(1, KV_HEADS * HEAD_SIZE, dtype=F32),
        ],
        1,
        keep=False,
    )(at, held(sums.reshape(n, dp, SUM_ROWS, HEAD_SIZE)))
    recv_k, recv_v = call(
        join_kv_kernel, [shape(ROWS, KV_HEADS * HEAD_SIZE)] * 2, 6, moved=2 << 20, keep=False
    )(at, kv_same, kv_other, r1s, r1x, r2s, r2x)
    (recv_q,) = call(
        join_q_kernel, [shape(ROWS, Q_HEADS * HEAD_SIZE)], 2, moved=1 << 20, keep=False
    )(at, gq_same, gq_other)
    return (recv_q[None, None], recv_k[None, None], recv_v[None, None], sum_q, sum_k, sum_v)


def solution(mesh):
    return jax.shard_map(
        body,
        mesh=mesh,
        in_specs=(
            P("dp", "section", "ctx", None),
            P("dp", "section", "ctx", None),
            P("dp", "section", "ctx", None),
            P("dp", "section", "ctx", None),
            P("dp", "section", "ctx", None),
            P("dp", "section", None, "ctx"),
            P("section", None),
            P("section", None),
            P("section", None),
        ),
        out_specs=(
            P("dp", "section", "ctx", None),
            P("dp", "section", "ctx", None),
            P("dp", "section", "ctx", None),
            P("section", None),
            P("section", None),
            P("section", None),
        ),
        check_vma=False,
    )
```

```python
import functools
import math

import jax
import jax.numpy as jnp
from jax import lax
from jax.experimental import pallas as pl
from jax.experimental.pallas import tpu as pltpu
from jax.sharding import PartitionSpec as P


HEAD_SIZE = 128
ROWS = 128
HALF = ROWS // 2
Q_HEADS = 16
KV_HEADS = 4
Q_OWN = Q_HEADS // 2
KV_OWN = KV_HEADS // 2
GROUP = Q_HEADS // KV_HEADS
SCALE = 1.0 / math.sqrt(HEAD_SIZE)
LOG2E = math.log2(math.e)
AT_Q = 0
AT_G = AT_Q + Q_OWN
AT_K = AT_G + Q_OWN
AT_V = AT_K + KV_OWN
AT_ROW = AT_V + KV_OWN
PACK = AT_ROW + 1
SUM_ROWS = 16
BF16 = jnp.bfloat16
F32 = jnp.float32
LOW = -1e30
KERNEL_VMEM = 24 << 20

SMEM = pl.BlockSpec(memory_space=pltpu.SMEM)
VMEM = pl.BlockSpec(memory_space=pltpu.VMEM)


def call(kernel, outs, n_in, flops=0, moved=0, keep=True, vmem=KERNEL_VMEM):
    keep = len(outs) if keep is True else int(keep)
    outs = [pltpu.VMEM(o.shape, o.dtype) for o in outs[:keep]] + outs[keep:]
    run = pl.pallas_call(
        kernel,
        out_shape=outs,
        in_specs=[SMEM] + [VMEM] * n_in,
        out_specs=[VMEM] * len(outs),
        compiler_params=pltpu.CompilerParams(vmem_limit_bytes=vmem),
        cost_estimate=pl.CostEstimate(flops=flops, bytes_accessed=moved, transcendentals=0),
    )
    return run


def held(x):
    return pltpu.with_memory_space_constraint(x, pltpu.VMEM)


def shape(*dims, dtype=BF16):
    return jax.ShapeDtypeStruct(dims, dtype)


def split3(x):
    a = x.astype(BF16)
    rest = x - a.astype(F32)
    b = rest.astype(BF16)
    return a, b, (rest - b.astype(F32)).astype(BF16)


def prep_kernel(at, q, k, v, o, g, lse, bq, bk, bv, own, send, kvz):
    core = at[0] % 2
    for pack, side in ((own, core), (send, 1 - core)):
        base = pl.multiple_of(side * (Q_OWN * HEAD_SIZE), Q_OWN * HEAD_SIZE)
        kv_base = pl.multiple_of(side * (KV_OWN * HEAD_SIZE), KV_OWN * HEAD_SIZE)
        deltas = []
        for h in range(Q_OWN):
            cols = pl.ds(base + h * HEAD_SIZE, HEAD_SIZE)
            pack[AT_Q + h] = (q[:, cols].astype(F32) + bq[:, cols].astype(F32)).astype(BF16)
            grad = g[:, cols]
            pack[AT_G + h] = grad
            deltas.append(
                jnp.sum(grad.astype(F32) * o[:, cols].astype(F32), axis=1, keepdims=True)
            )
        for h in range(KV_OWN):
            cols = pl.ds(kv_base + h * HEAD_SIZE, HEAD_SIZE)
            kb = (k[:, cols].astype(F32) + bk[:, cols].astype(F32)).astype(BF16)
            vb = (v[:, cols].astype(F32) + bv[:, cols].astype(F32)).astype(BF16)
            pack[AT_K + h] = kb
            pack[AT_V + h] = vb
            to = 0 if pack is own else 1
            for late in range(2):
                rows = slice(late * HALF, (late + 1) * HALF)
                kvz[to, late, h] = kb[rows]
                kvz[to, late, KV_OWN + h] = vb[rows]
        delta = jnp.concatenate(deltas + [jnp.zeros((ROWS, HEAD_SIZE - Q_OWN), F32)], axis=1).T
        heads = pl.ds(pl.multiple_of(side * Q_OWN, Q_OWN), Q_OWN)
        stats = jnp.concatenate(
            [p.astype(F32) for p in split3(lse[heads, :])]
            + [p.astype(F32) for p in split3(delta[:Q_OWN])]
            + [jnp.zeros((ROWS - 6 * Q_OWN, HEAD_SIZE), F32)],
            axis=0,
        )
        pack[AT_ROW] = stats.astype(BF16)


def row_stats(own, recv):
    def one(pack):
        s = pack[AT_ROW].astype(F32)
        n = Q_OWN
        lse = (s[:n] + s[n : 2 * n]) + s[2 * n : 3 * n]
        delta = (s[3 * n : 4 * n] + s[4 * n : 5 * n]) + s[5 * n : 6 * n]
        return lse * LOG2E, delta

    (la, da), (lb, db) = one(own), one(recv)
    return jnp.concatenate([la, lb], axis=1), jnp.concatenate([da, db], axis=1)


def positions(index, dim, ctx_count, alternate):
    i = lax.broadcasted_iota(jnp.int32, (2 * ROWS, 2 * ROWS), dim)
    part = i // HALF
    late = part // 2 if alternate else part % 2
    other = part % 2 if alternate else part // 2
    block = jnp.where(other == 1, index + 1 - 2 * (index % 2), index)
    half = jnp.where(late == 1, 2 * ctx_count - 1 - block, block)
    return half * HALF + i % HALF


def head_terms(q, g, k, v, bias, lse, delta):
    s = lax.dot_general(k, q, (((1,), (1,)), ((), ())), preferred_element_type=F32)
    dp = lax.dot_general(v, g, (((1,), (1,)), ((), ())), preferred_element_type=F32)
    p = jnp.exp2(s * (SCALE * LOG2E) + (bias - lse))
    ds = (p * (dp - delta)).astype(BF16)
    p = p.astype(BF16)
    gv = jnp.dot(p, g, preferred_element_type=F32)
    gk = jnp.dot(ds, q, preferred_element_type=F32)
    gq = lax.dot_general(ds, k, (((0,), (0,)), ((), ())), preferred_element_type=F32)
    return gq, gk, gv


def local_kernel(at, own, recv, gq_out, same, other, kv_sums, *, ctx_count):
    kpos = positions(at[0], 0, ctx_count, False)
    qpos = positions(at[0], 1, ctx_count, False)
    bias = jnp.where(kpos <= qpos, 0.0, LOW)
    lse, delta = row_stats(own, recv)
    for kv in range(KV_OWN):
        k = jnp.concatenate([own[AT_K + kv], recv[AT_K + kv]], axis=0)
        v = jnp.concatenate([own[AT_V + kv], recv[AT_V + kv]], axis=0)
        gk = gv = None
        for j in range(GROUP):
            h = kv * GROUP + j
            q = jnp.concatenate([own[AT_Q + h], recv[AT_Q + h]], axis=0)
            g = jnp.concatenate([own[AT_G + h], recv[AT_G + h]], axis=0)
            tq, tk, tv = head_terms(q, g, k, v, bias, lse[h : h + 1], delta[h : h + 1])
            gq_out[h] = tq
            gk = tk if gk is None else gk + tk
            gv = tv if gv is None else gv + tv
        for row, t in ((kv, gk * SCALE), (KV_OWN + kv, gv)):
            same[row] = t[:ROWS]
            other[row] = t[ROWS:]
            kv_sums[row : row + 1, :] = jnp.sum(t, axis=0, keepdims=True)


def remote_kernel(
    at, own, recv, far, cross, gq_in, kv_sums, gq_same, gq_other, r1s, r1x, r2s, r2x, sums, *, ctx_count
):
    far_kv = (far.at[0, 0], cross.at[0], far.at[0, 1], cross.at[1])
    totals = []
    far_index = (at[0] + ctx_count // 2) % ctx_count
    kpos = positions(far_index, 0, ctx_count, True)
    qpos = positions(at[0], 1, ctx_count, False)
    bias = jnp.where(kpos <= qpos, 0.0, LOW)
    lse, delta = row_stats(own, recv)
    for kv in range(KV_OWN):
        k = jnp.concatenate([r[kv] for r in far_kv], axis=0)
        v = jnp.concatenate([r[KV_OWN + kv] for r in far_kv], axis=0)
        gk = gv = None
        for j in range(GROUP):
            h = kv * GROUP + j
            q = jnp.concatenate([own[AT_Q + h], recv[AT_Q + h]], axis=0)
            g = jnp.concatenate([own[AT_G + h], recv[AT_G + h]], axis=0)
            tq, tk, tv = head_terms(q, g, k, v, bias, lse[h : h + 1], delta[h : h + 1])
            gq = (gq_in[h] + tq) * SCALE
            gq_same[h] = gq[:ROWS].astype(BF16)
            gq_other[h] = gq[ROWS:].astype(BF16)
            totals.append((h, jnp.sum(gq, axis=0, keepdims=True)))
            gk = tk if gk is None else gk + tk
            gv = tv if gv is None else gv + tv
        for row, t in ((kv, gk * SCALE), (KV_OWN + kv, gv)):
            for part, out in enumerate((r1s, r1x, r2s, r2x)):
                out[row] = t[part * HALF : (part + 1) * HALF]
            total = jnp.sum(t, axis=0, keepdims=True) + kv_sums[row : row + 1, :]
            totals.append((Q_OWN + row, total))
    pad = SUM_ROWS - len(totals)
    totals = [t for _, t in sorted(totals, key=lambda t: t[0])] + [jnp.zeros((pad, HEAD_SIZE), F32)]
    sums[...] = jnp.concatenate(totals, axis=0)


def cross_kernel(at, far, out):
    out[...] = far[1]


def join_q_kernel(at, same, other, out):
    core = at[0] % 2
    for part, side in ((same, core), (other, 1 - core)):
        base = pl.multiple_of(side * (Q_OWN * HEAD_SIZE), Q_OWN * HEAD_SIZE)
        for h in range(Q_OWN):
            out[:, pl.ds(base + h * HEAD_SIZE, HEAD_SIZE)] = part[h]


def join_kv_kernel(at, same, other, r1s, r1x, r2s, r2x, out_k, out_v):
    core = at[0] % 2
    for near, first, second, side in ((same, r1s, r2s, core), (other, r1x, r2x, 1 - core)):
        base = pl.multiple_of(side * (KV_OWN * HEAD_SIZE), KV_OWN * HEAD_SIZE)
        for h in range(KV_OWN):
            cols = pl.ds(base + h * HEAD_SIZE, HEAD_SIZE)
            for out, i in ((out_k, h), (out_v, KV_OWN + h)):
                out[:HALF, cols] = (near[i, :HALF] + first[i]).astype(BF16)
                out[HALF:, cols] = (near[i, HALF:] + second[i]).astype(BF16)


def pair_sums_kernel(at, mine, theirs, out):
    out[...] = jnp.broadcast_to((mine[...] + theirs[...])[None], out.shape)


def replica_sums_kernel(at, parts, out):
    total = parts[0]
    for r in range(1, parts.shape[0]):
        total = total + parts[r]
    out[...] = total


def join_sums_kernel(at, same, other, out_q, out_k, out_v):
    core = at[0] % 2
    for part, side in ((same, core), (other, 1 - core)):
        base = pl.multiple_of(side * (Q_OWN * HEAD_SIZE), Q_OWN * HEAD_SIZE)
        kv_base = pl.multiple_of(side * (KV_OWN * HEAD_SIZE), KV_OWN * HEAD_SIZE)
        for h in range(Q_OWN):
            out_q[:, pl.ds(base + h * HEAD_SIZE, HEAD_SIZE)] = part[h : h + 1, :]
        for h in range(KV_OWN):
            cols = pl.ds(kv_base + h * HEAD_SIZE, HEAD_SIZE)
            row = Q_OWN + h
            out_k[:, cols] = part[row : row + 1, :]
            row += KV_OWN
            out_v[:, cols] = part[row : row + 1, :]


def swapped(value, axis, bit):
    size = lax.axis_size(axis)
    return lax.ppermute(value, axis, [(i, i ^ bit) for i in range(size)])


def body(q_in, k_in, v_in, o_in, g_in, lse, bq, bk, bv):
    n = lax.axis_size("ctx")
    at = lax.axis_index("ctx").astype(jnp.int32).reshape(1)
    chips = n // 2
    blocks = lambda count, rows=ROWS, dtype=BF16: shape(count, rows, HEAD_SIZE, dtype=dtype)

    dp = lax.axis_size("dp")
    own, send, kvz = call(
        prep_kernel,
        [blocks(PACK), blocks(PACK), shape(2, 2, 2 * KV_OWN, HALF, HEAD_SIZE)],
        9,
        moved=4 << 20,
        vmem=60 << 20,
    )(at, q_in[0, 0], k_in[0, 0], v_in[0, 0], o_in[0, 0], g_in[0, 0], lse[0, 0], bq, bk, bv)

    far = held(swapped(kvz, "ctx", chips))
    recv = held(swapped(send, "ctx", 1))
    own = held(own)

    gq, kv_same, kv_other, kv_sums = call(
        functools.partial(local_kernel, ctx_count=n),
        [blocks(Q_OWN, 2 * ROWS, F32)]
        + [blocks(2 * KV_OWN, ROWS, F32)] * 2
        + [shape(2 * KV_OWN, HEAD_SIZE, dtype=F32)],
        2,
        flops=700_000_000,
        moved=3 << 20,
    )(at, own, recv)

    def before(x, bit, senders=range(n)):
        pairs = []
        for s in range(1, lax.axis_size("section")):
            pairs += [(s * n + c, (s - 1) * n + (c ^ bit)) for c in senders]
        return held(lax.ppermute(x, ("section", "ctx"), pairs))

    kv_same, kv_other = before(kv_same, 0), before(kv_other, 1)
    (cross,) = call(cross_kernel, [shape(2, 2 * KV_OWN, HALF, HEAD_SIZE)], 1)(at, far)
    cross = held(swapped(cross, "ctx", 1))
    gq_same, gq_other, r1s, r1x, r2s, r2x, sums = call(
        functools.partial(remote_kernel, ctx_count=n),
        [blocks(Q_OWN)] * 2
        + [blocks(2 * KV_OWN, HALF, F32)] * 4
        + [shape(SUM_ROWS, HEAD_SIZE, dtype=F32)],
        6,
        flops=700_000_000,
        moved=4 << 20,
    )(at, own, recv, far, cross, held(gq), held(kv_sums))

    r2s = before(r2s, chips, range(chips))
    r2x = before(r2x, chips + 1, range(chips))
    r1s, r1x = before(r1s, chips), before(r1x, chips + 1)
    gq_same, gq_other = before(gq_same, 0), before(gq_other, 1)
    far_sums = held(swapped(sums, "ctx", chips))
    (copies,) = call(
        pair_sums_kernel, [shape(dp, SUM_ROWS, HEAD_SIZE, dtype=F32)], 2, keep=False
    )(at, held(sums), far_sums)
    copies = held(lax.all_to_all(copies, "dp", 0, 0, tiled=True))
    (sums,) = call(replica_sums_kernel, [shape(SUM_ROWS, HEAD_SIZE, dtype=F32)], 1)(at, copies)
    sum_q, sum_k, sum_v = call(
        join_sums_kernel,
        [
            shape(1, Q_HEADS * HEAD_SIZE, dtype=F32),
            shape(1, KV_HEADS * HEAD_SIZE, dtype=F32),
            shape(1, KV_HEADS * HEAD_SIZE, dtype=F32),
        ],
        2,
        keep=False,
    )(at, held(sums), held(swapped(sums, "ctx", 1)))
    recv_k, recv_v = call(
        join_kv_kernel, [shape(ROWS, KV_HEADS * HEAD_SIZE)] * 2, 6, moved=2 << 20, keep=False
    )(at, kv_same, kv_other, r1s, r1x, r2s, r2x)
    (recv_q,) = call(
        join_q_kernel, [shape(ROWS, Q_HEADS * HEAD_SIZE)], 2, moved=1 << 20, keep=False
    )(at, gq_same, gq_other)
    return (recv_q[None, None], recv_k[None, None], recv_v[None, None], sum_q, sum_k, sum_v)


def solution(mesh):
    return jax.shard_map(
        body,
        mesh=mesh,
        in_specs=(
            P("dp", "section", "ctx", None),
            P("dp", "section", "ctx", None),
            P("dp", "section", "ctx", None),
            P("dp", "section", "ctx", None),
            P("dp", "section", "ctx", None),
            P("dp", "section", None, "ctx"),
            P("section", None),
            P("section", None),
            P("section", None),
        ),
        out_specs=(
            P("dp", "section", "ctx", None),
            P("dp", "section", "ctx", None),
            P("dp", "section", "ctx", None),
            P("section", None),
            P("section", None),
            P("section", None),
        ),
        check_vma=False,
    )
```

```python
import functools
import math

import jax
import jax.numpy as jnp
from jax import lax
from jax.experimental import pallas as pl
from jax.experimental.pallas import tpu as pltpu
from jax.sharding import PartitionSpec as P


HEAD_SIZE = 128
ROWS = 128
HALF = ROWS // 2
Q_HEADS = 16
KV_HEADS = 4
Q_OWN = Q_HEADS // 2
KV_OWN = KV_HEADS // 2
GROUP = Q_HEADS // KV_HEADS
SCALE = 1.0 / math.sqrt(HEAD_SIZE)
LOG2E = math.log2(math.e)
AT_Q = 0
AT_G = AT_Q + Q_OWN
AT_K = AT_G + Q_OWN
AT_V = AT_K + KV_OWN
AT_ROW = AT_V + KV_OWN
PACK = AT_ROW + 1
SUM_ROWS = 16
BF16 = jnp.bfloat16
F32 = jnp.float32
LOW = -1e30
KERNEL_VMEM = 24 << 20

SMEM = pl.BlockSpec(memory_space=pltpu.SMEM)
VMEM = pl.BlockSpec(memory_space=pltpu.VMEM)


def call(kernel, outs, n_in, flops=0, moved=0, keep=True, vmem=KERNEL_VMEM):
    keep = len(outs) if keep is True else int(keep)
    outs = [pltpu.VMEM(o.shape, o.dtype) for o in outs[:keep]] + outs[keep:]
    run = pl.pallas_call(
        kernel,
        out_shape=outs,
        in_specs=[SMEM] + [VMEM] * n_in,
        out_specs=[VMEM] * len(outs),
        compiler_params=pltpu.CompilerParams(vmem_limit_bytes=vmem),
        cost_estimate=pl.CostEstimate(flops=flops, bytes_accessed=moved, transcendentals=0),
    )
    return run


def held(x):
    return pltpu.with_memory_space_constraint(x, pltpu.VMEM)


def shape(*dims, dtype=BF16):
    return jax.ShapeDtypeStruct(dims, dtype)


def split3(x):
    a = x.astype(BF16)
    rest = x - a.astype(F32)
    b = rest.astype(BF16)
    return a, b, (rest - b.astype(F32)).astype(BF16)


def prep_kernel(at, q, k, v, o, g, lse, bq, bk, bv, own, send, kvz, *, ctx_count):
    core = at[0] % 2
    low_chip = at[0] < ctx_count // 2
    for pack, side in ((own, core), (send, 1 - core)):
        base = pl.multiple_of(side * (Q_OWN * HEAD_SIZE), Q_OWN * HEAD_SIZE)
        kv_base = pl.multiple_of(side * (KV_OWN * HEAD_SIZE), KV_OWN * HEAD_SIZE)
        deltas = []
        for h in range(Q_OWN):
            cols = pl.ds(base + h * HEAD_SIZE, HEAD_SIZE)
            pack[AT_Q + h] = (q[:, cols].astype(F32) + bq[:, cols].astype(F32)).astype(BF16)
            grad = g[:, cols]
            pack[AT_G + h] = grad
            deltas.append(
                jnp.sum(grad.astype(F32) * o[:, cols].astype(F32), axis=1, keepdims=True)
            )
        to = 0 if pack is own else 1
        for h in range(KV_OWN):
            cols = pl.ds(kv_base + h * HEAD_SIZE, HEAD_SIZE)
            kb = (k[:, cols].astype(F32) + bk[:, cols].astype(F32)).astype(BF16)
            vb = (v[:, cols].astype(F32) + bv[:, cols].astype(F32)).astype(BF16)
            pack[AT_K + h] = kb
            pack[AT_V + h] = vb
            for i, t in ((h, kb), (KV_OWN + h, vb)):
                kvz[to, 0, i] = t[:HALF]
                kvz[to, 1, i] = jnp.where(low_chip, pack[AT_G + i, HALF:], t[HALF:])
        delta = jnp.concatenate(deltas + [jnp.zeros((ROWS, HEAD_SIZE - Q_OWN), F32)], axis=1).T
        heads = pl.ds(pl.multiple_of(side * Q_OWN, Q_OWN), Q_OWN)
        stats = jnp.concatenate(
            [p.astype(F32) for p in split3(lse[heads, :])]
            + [p.astype(F32) for p in split3(delta[:Q_OWN])]
            + [jnp.zeros((ROWS - 6 * Q_OWN, HEAD_SIZE), F32)],
            axis=0,
        )
        pack[AT_ROW] = stats.astype(BF16)


def pack_stats(s):
    n = Q_OWN
    lse = (s[:n] + s[n : 2 * n]) + s[2 * n : 3 * n]
    delta = (s[3 * n : 4 * n] + s[4 * n : 5 * n]) + s[5 * n : 6 * n]
    return lse * LOG2E, delta


def row_stats(own, recv):
    (la, da), (lb, db) = (pack_stats(p[AT_ROW].astype(F32)) for p in (own, recv))
    return jnp.concatenate([la, lb], axis=1), jnp.concatenate([da, db], axis=1)


def positions(index, dim, ctx_count, alternate):
    i = lax.broadcasted_iota(jnp.int32, (2 * ROWS, 2 * ROWS), dim)
    part = i // HALF
    late = part // 2 if alternate else part % 2
    other = part % 2 if alternate else part // 2
    block = jnp.where(other == 1, index + 1 - 2 * (index % 2), index)
    half = jnp.where(late == 1, 2 * ctx_count - 1 - block, block)
    return half * HALF + i % HALF


def head_terms(q, g, k, v, bias, lse, delta):
    s = lax.dot_general(k, q, (((1,), (1,)), ((), ())), preferred_element_type=F32)
    dp = lax.dot_general(v, g, (((1,), (1,)), ((), ())), preferred_element_type=F32)
    p = jnp.exp2(s * (SCALE * LOG2E) + (bias - lse))
    ds = (p * (dp - delta)).astype(BF16)
    p = p.astype(BF16)
    gv = jnp.dot(p, g, preferred_element_type=F32)
    gk = jnp.dot(ds, q, preferred_element_type=F32)
    gq = lax.dot_general(ds, k, (((0,), (0,)), ((), ())), preferred_element_type=F32)
    return gq, gk, gv


def local_kernel(at, own, recv, gq_out, gkv_out, kv_sums, q_late, *, ctx_count):
    kpos = positions(at[0], 0, ctx_count, False)
    qpos = positions(at[0], 1, ctx_count, False)
    bias = jnp.where(kpos <= qpos, 0.0, LOW)
    lse, delta = row_stats(own, recv)
    for kv in range(KV_OWN):
        k = jnp.concatenate([own[AT_K + kv], recv[AT_K + kv]], axis=0)
        v = jnp.concatenate([own[AT_V + kv], recv[AT_V + kv]], axis=0)
        gk = gv = None
        for j in range(GROUP):
            h = kv * GROUP + j
            q = jnp.concatenate([own[AT_Q + h], recv[AT_Q + h]], axis=0)
            g = jnp.concatenate([own[AT_G + h], recv[AT_G + h]], axis=0)
            tq, tk, tv = head_terms(q, g, k, v, bias, lse[h : h + 1], delta[h : h + 1])
            gq_out[h] = tq
            gk = tk if gk is None else gk + tk
            gv = tv if gv is None else gv + tv
        for row, t in ((kv, gk * SCALE), (KV_OWN + kv, gv)):
            gkv_out[row] = t
            kv_sums[row : row + 1, :] = jnp.sum(t, axis=0, keepdims=True)


    for h in range(GROUP):
        q_late[h, :HALF] = own[AT_Q + h, HALF:]
        q_late[h, HALF:] = recv[AT_Q + h, HALF:]
    q_late[GROUP, :HALF] = own[AT_ROW, :HALF]
    q_late[GROUP, HALF:] = recv[AT_ROW, :HALF]


def extra_kernel(at, own, recv, far, cross, q_late, out, *, ctx_count):
    k = jnp.concatenate([own[AT_K], recv[AT_K]], axis=0)
    v = jnp.concatenate([own[AT_V], recv[AT_V]], axis=0)
    lse, delta = (
        jnp.concatenate([a[:, HALF:], b[:, HALF:]], axis=1)
        for a, b in zip(
            pack_stats(q_late[GROUP, :HALF].astype(F32)), pack_stats(q_late[GROUP, HALF:].astype(F32))
        )
    )
    gk = gv = None
    for h in range(GROUP):
        g = jnp.concatenate([far[0, 1, h], cross[1, h]], axis=0)
        _, tk, tv = head_terms(q_late[h], g, k, v, 0.0, lse[h : h + 1], delta[h : h + 1])
        gk = tk if gk is None else gk + tk
        gv = tv if gv is None else gv + tv
    high_chip = at[0] >= ctx_count // 2
    out[0] = jnp.where(high_chip, gk * SCALE, 0.0)
    out[1] = jnp.where(high_chip, gv, 0.0)


def remote_kernel(
    at, own, recv, far, cross, gq_in, kv_sums, gq_same, gq_other, r, sums, *, ctx_count
):
    low_chip = at[0] < ctx_count // 2
    terms = []
    far_kv = (far.at[0, 0], cross.at[0], far.at[0, 1], cross.at[1])
    totals = []
    far_index = (at[0] + ctx_count // 2) % ctx_count
    kpos = positions(far_index, 0, ctx_count, True)
    qpos = positions(at[0], 1, ctx_count, False)
    bias = jnp.where(kpos <= qpos, 0.0, LOW)
    lse, delta = row_stats(own, recv)
    for kv in range(KV_OWN):
        k = jnp.concatenate([r[kv] for r in far_kv], axis=0)
        v = jnp.concatenate([r[KV_OWN + kv] for r in far_kv], axis=0)
        gk = gv = None
        for j in range(GROUP):
            h = kv * GROUP + j
            q = jnp.concatenate([own[AT_Q + h], recv[AT_Q + h]], axis=0)
            g = jnp.concatenate([own[AT_G + h], recv[AT_G + h]], axis=0)
            tq, tk, tv = head_terms(q, g, k, v, bias, lse[h : h + 1], delta[h : h + 1])
            gq = (gq_in[h] + tq) * SCALE
            gq_same[h] = gq[:ROWS].astype(BF16)
            gq_other[h] = gq[ROWS:].astype(BF16)
            totals.append((h, jnp.sum(gq, axis=0, keepdims=True)))
            gk = tk if gk is None else gk + tk
            gv = tv if gv is None else gv + tv
        for row, t in ((kv, gk * SCALE), (KV_OWN + kv, gv)):
            terms.append((row, t))
            total = jnp.sum(t, axis=0, keepdims=True) + kv_sums[row : row + 1, :]
            totals.append((Q_OWN + row, total))
    terms = [t for _, t in sorted(terms, key=lambda t: t[0])]
    for i in range(2 * KV_OWN):
        late = i % 2
        low = terms[KV_OWN * (i // 2) + 1][late * ROWS : (late + 1) * ROWS]
        r[i] = jnp.where(low_chip, low, terms[i][:ROWS])
    pad = SUM_ROWS - len(totals)
    totals = [t for _, t in sorted(totals, key=lambda t: t[0])] + [jnp.zeros((pad, HEAD_SIZE), F32)]
    sums[...] = jnp.concatenate(totals, axis=0)


def cross_kernel(at, far, out):
    out[...] = far[1]


def kv_kernel(at, gkv, extra, r, same, other, *, ctx_count):
    low_chip = at[0] < ctx_count // 2
    for i in range(2 * KV_OWN):
        for late in range(2):
            from_low = r[KV_OWN * (i // KV_OWN) + late] if i % KV_OWN else None
            from_high = r[i] if late == 0 else None
            zero = jnp.zeros((ROWS, HEAD_SIZE), F32)
            got = jnp.where(
                low_chip,
                zero if from_high is None else from_high,
                zero if from_low is None else from_low,
            )
            for out, block in ((same, 0), (other, 1)):
                rows = slice(block * ROWS + late * HALF, block * ROWS + (late + 1) * HALF)
                t = gkv[i, rows] + got[block * HALF : (block + 1) * HALF]
                if i % KV_OWN == 0:
                    t = t + extra[i // KV_OWN, rows]
                out[i, late * HALF : (late + 1) * HALF] = t.astype(BF16)


def join_q_kernel(at, same, other, out):
    core = at[0] % 2
    for part, side in ((same, core), (other, 1 - core)):
        base = pl.multiple_of(side * (Q_OWN * HEAD_SIZE), Q_OWN * HEAD_SIZE)
        for h in range(Q_OWN):
            out[:, pl.ds(base + h * HEAD_SIZE, HEAD_SIZE)] = part[h]


def join_kv_kernel(at, same, other, out_k, out_v):
    core = at[0] % 2
    for part, side in ((same, core), (other, 1 - core)):
        base = pl.multiple_of(side * (KV_OWN * HEAD_SIZE), KV_OWN * HEAD_SIZE)
        for h in range(KV_OWN):
            cols = pl.ds(base + h * HEAD_SIZE, HEAD_SIZE)
            out_k[:, cols] = part[h]
            out_v[:, cols] = part[KV_OWN + h]


def pair_sums_kernel(at, mine, theirs, out):
    out[...] = jnp.broadcast_to((mine[...] + theirs[...])[None], out.shape)


def replica_sums_kernel(at, parts, out):
    total = parts[0]
    for r in range(1, parts.shape[0]):
        total = total + parts[r]
    out[...] = total


def join_sums_kernel(at, same, other, out_q, out_k, out_v):
    core = at[0] % 2
    for part, side in ((same, core), (other, 1 - core)):
        base = pl.multiple_of(side * (Q_OWN * HEAD_SIZE), Q_OWN * HEAD_SIZE)
        kv_base = pl.multiple_of(side * (KV_OWN * HEAD_SIZE), KV_OWN * HEAD_SIZE)
        for h in range(Q_OWN):
            out_q[:, pl.ds(base + h * HEAD_SIZE, HEAD_SIZE)] = part[h : h + 1, :]
        for h in range(KV_OWN):
            cols = pl.ds(kv_base + h * HEAD_SIZE, HEAD_SIZE)
            row = Q_OWN + h
            out_k[:, cols] = part[row : row + 1, :]
            row += KV_OWN
            out_v[:, cols] = part[row : row + 1, :]


def swapped(value, axis, bit):
    size = lax.axis_size(axis)
    return lax.ppermute(value, axis, [(i, i ^ bit) for i in range(size)])


def body(q_in, k_in, v_in, o_in, g_in, lse, bq, bk, bv):
    n = lax.axis_size("ctx")
    at = lax.axis_index("ctx").astype(jnp.int32).reshape(1)
    chips = n // 2
    blocks = lambda count, rows=ROWS, dtype=BF16: shape(count, rows, HEAD_SIZE, dtype=dtype)

    dp = lax.axis_size("dp")
    own, send, kvz = call(
        functools.partial(prep_kernel, ctx_count=n),
        [blocks(PACK), blocks(PACK), shape(2, 2, 2 * KV_OWN, HALF, HEAD_SIZE)],
        9,
        moved=4 << 20,
        vmem=60 << 20,
    )(at, q_in[0, 0], k_in[0, 0], v_in[0, 0], o_in[0, 0], g_in[0, 0], lse[0, 0], bq, bk, bv)

    far = held(swapped(kvz, "ctx", chips))
    recv = held(swapped(send, "ctx", 1))
    own = held(own)

    gq, gkv, kv_sums, q_late = call(
        functools.partial(local_kernel, ctx_count=n),
        [blocks(Q_OWN, 2 * ROWS, F32), blocks(2 * KV_OWN, 2 * ROWS, F32)]
        + [shape(2 * KV_OWN, HEAD_SIZE, dtype=F32), blocks(GROUP + 1)],
        2,
        flops=700_000_000,
        moved=3 << 20,
    )(at, own, recv)
    q_late = held(lax.ppermute(q_late, "ctx", [(i, i + chips) for i in range(chips)]))

    def before(x, bit):
        pairs = []
        for s in range(1, lax.axis_size("section")):
            pairs += [(s * n + c, (s - 1) * n + (c ^ bit)) for c in range(n)]
        return held(lax.ppermute(x, ("section", "ctx"), pairs))

    (cross,) = call(cross_kernel, [shape(2, 2 * KV_OWN, HALF, HEAD_SIZE)], 1)(at, far)
    cross = held(swapped(cross, "ctx", 1))
    gq_same, gq_other, r, sums = call(
        functools.partial(remote_kernel, ctx_count=n),
        [blocks(Q_OWN)] * 2
        + [blocks(2 * KV_OWN, ROWS, F32), shape(SUM_ROWS, HEAD_SIZE, dtype=F32)],
        6,
        flops=700_000_000,
        moved=4 << 20,
    )(at, own, recv, far, cross, held(gq), held(kv_sums))

    r = held(swapped(r, "ctx", chips))
    gq_same, gq_other = before(gq_same, 0), before(gq_other, 1)
    (extra,) = call(
        functools.partial(extra_kernel, ctx_count=n),
        [blocks(2, 2 * ROWS, F32)],
        5,
        flops=150_000_000,
        moved=1 << 20,
    )(at, own, recv, far, cross, q_late)
    kv_same, kv_other = call(
        functools.partial(kv_kernel, ctx_count=n), [blocks(2 * KV_OWN)] * 2, 3, moved=2 << 20
    )(at, held(gkv), held(extra), r)
    kv_same, kv_other = before(kv_same, 0), before(kv_other, 1)
    far_sums = held(swapped(sums, "ctx", chips))
    (copies,) = call(
        pair_sums_kernel, [shape(dp, SUM_ROWS, HEAD_SIZE, dtype=F32)], 2, keep=False
    )(at, held(sums), far_sums)
    copies = held(lax.all_to_all(copies, "dp", 0, 0, tiled=True))
    (sums,) = call(replica_sums_kernel, [shape(SUM_ROWS, HEAD_SIZE, dtype=F32)], 1)(at, copies)
    sum_q, sum_k, sum_v = call(
        join_sums_kernel,
        [
            shape(1, Q_HEADS * HEAD_SIZE, dtype=F32),
            shape(1, KV_HEADS * HEAD_SIZE, dtype=F32),
            shape(1, KV_HEADS * HEAD_SIZE, dtype=F32),
        ],
        2,
        keep=False,
    )(at, held(sums), held(swapped(sums, "ctx", 1)))
    recv_k, recv_v = call(
        join_kv_kernel, [shape(ROWS, KV_HEADS * HEAD_SIZE)] * 2, 2, moved=1 << 19, keep=False
    )(at, kv_same, kv_other)
    (recv_q,) = call(
        join_q_kernel, [shape(ROWS, Q_HEADS * HEAD_SIZE)], 2, moved=1 << 20, keep=False
    )(at, gq_same, gq_other)
    return (recv_q[None, None], recv_k[None, None], recv_v[None, None], sum_q, sum_k, sum_v)


def solution(mesh):
    return jax.shard_map(
        body,
        mesh=mesh,
        in_specs=(
            P("dp", "section", "ctx", None),
            P("dp", "section", "ctx", None),
            P("dp", "section", "ctx", None),
            P("dp", "section", "ctx", None),
            P("dp", "section", "ctx", None),
            P("dp", "section", None, "ctx"),
            P("section", None),
            P("section", None),
            P("section", None),
        ),
        out_specs=(
            P("dp", "section", "ctx", None),
            P("dp", "section", "ctx", None),
            P("dp", "section", "ctx", None),
            P("section", None),
            P("section", None),
            P("section", None),
        ),
        check_vma=False,
    )
```

```python
import functools
import math

import jax
import jax.numpy as jnp
from jax import lax
from jax.experimental import pallas as pl
from jax.experimental.pallas import tpu as pltpu
from jax.sharding import PartitionSpec as P


HEAD_SIZE = 128
ROWS = 128
HALF = ROWS // 2
Q_HEADS = 16
KV_HEADS = 4
Q_OWN = Q_HEADS // 2
KV_OWN = KV_HEADS // 2
GROUP = Q_HEADS // KV_HEADS
SCALE = 1.0 / math.sqrt(HEAD_SIZE)
LOG2E = math.log2(math.e)
AT_Q = 0
AT_G = AT_Q + Q_OWN
AT_K = AT_G + Q_OWN
AT_V = AT_K + KV_OWN
AT_ROW = AT_V + KV_OWN
PACK = AT_ROW + 1
SUM_ROWS = 16
BF16 = jnp.bfloat16
F32 = jnp.float32
LOW = -1e30
KERNEL_VMEM = 24 << 20

SMEM = pl.BlockSpec(memory_space=pltpu.SMEM)
VMEM = pl.BlockSpec(memory_space=pltpu.VMEM)


def call(kernel, outs, n_in, flops=0, moved=0, keep=True, vmem=KERNEL_VMEM):
    keep = len(outs) if keep is True else int(keep)
    outs = [pltpu.VMEM(o.shape, o.dtype) for o in outs[:keep]] + outs[keep:]
    run = pl.pallas_call(
        kernel,
        out_shape=outs,
        in_specs=[SMEM] + [VMEM] * n_in,
        out_specs=[VMEM] * len(outs),
        compiler_params=pltpu.CompilerParams(vmem_limit_bytes=vmem),
        cost_estimate=pl.CostEstimate(flops=flops, bytes_accessed=moved, transcendentals=0),
    )
    return run


def held(x):
    return pltpu.with_memory_space_constraint(x, pltpu.VMEM)


def shape(*dims, dtype=BF16):
    return jax.ShapeDtypeStruct(dims, dtype)


def split3(x):
    a = x.astype(BF16)
    rest = x - a.astype(F32)
    b = rest.astype(BF16)
    return a, b, (rest - b.astype(F32)).astype(BF16)


def prep_kernel(at, q, k, v, o, g, lse, bq, bk, bv, own, send, kvz, *, ctx_count):
    core = at[0] % 2
    low_chip = at[0] < ctx_count // 2
    for pack, side in ((own, core), (send, 1 - core)):
        base = pl.multiple_of(side * (Q_OWN * HEAD_SIZE), Q_OWN * HEAD_SIZE)
        kv_base = pl.multiple_of(side * (KV_OWN * HEAD_SIZE), KV_OWN * HEAD_SIZE)
        deltas = []
        for h in range(Q_OWN):
            cols = pl.ds(base + h * HEAD_SIZE, HEAD_SIZE)
            pack[AT_Q + h] = (q[:, cols].astype(F32) + bq[:, cols].astype(F32)).astype(BF16)
            grad = g[:, cols]
            pack[AT_G + h] = grad
            deltas.append(
                jnp.sum(grad.astype(F32) * o[:, cols].astype(F32), axis=1, keepdims=True)
            )
        to = 0 if pack is own else 1
        for h in range(KV_OWN):
            cols = pl.ds(kv_base + h * HEAD_SIZE, HEAD_SIZE)
            kb = (k[:, cols].astype(F32) + bk[:, cols].astype(F32)).astype(BF16)
            vb = (v[:, cols].astype(F32) + bv[:, cols].astype(F32)).astype(BF16)
            pack[AT_K + h] = kb
            pack[AT_V + h] = vb
            for i, t in ((h, kb), (KV_OWN + h, vb)):
                kvz[to, 0, i] = t[:HALF]
                kvz[to, 1, i] = jnp.where(low_chip, pack[AT_G + i, HALF:], t[HALF:])
        delta = jnp.concatenate(deltas + [jnp.zeros((ROWS, HEAD_SIZE - Q_OWN), F32)], axis=1).T
        heads = pl.ds(pl.multiple_of(side * Q_OWN, Q_OWN), Q_OWN)
        stats = jnp.concatenate(
            [p.astype(F32) for p in split3(lse[heads, :])]
            + [p.astype(F32) for p in split3(delta[:Q_OWN])]
            + [jnp.zeros((ROWS - 6 * Q_OWN, HEAD_SIZE), F32)],
            axis=0,
        )
        pack[AT_ROW] = stats.astype(BF16)


def pack_stats(s):
    n = Q_OWN
    lse = (s[:n] + s[n : 2 * n]) + s[2 * n : 3 * n]
    delta = (s[3 * n : 4 * n] + s[4 * n : 5 * n]) + s[5 * n : 6 * n]
    return lse * LOG2E, delta


def row_stats(own, recv):
    (la, da), (lb, db) = (pack_stats(p[AT_ROW].astype(F32)) for p in (own, recv))
    return jnp.concatenate([la, lb], axis=1), jnp.concatenate([da, db], axis=1)


def positions(index, dim, ctx_count, alternate):
    i = lax.broadcasted_iota(jnp.int32, (2 * ROWS, 2 * ROWS), dim)
    part = i // HALF
    late = part // 2 if alternate else part % 2
    other = part % 2 if alternate else part // 2
    block = jnp.where(other == 1, index + 1 - 2 * (index % 2), index)
    half = jnp.where(late == 1, 2 * ctx_count - 1 - block, block)
    return half * HALF + i % HALF


def head_terms(q, g, k, v, bias, lse, delta):
    s = lax.dot_general(k, q, (((1,), (1,)), ((), ())), preferred_element_type=F32)
    dp = lax.dot_general(v, g, (((1,), (1,)), ((), ())), preferred_element_type=F32)
    p = jnp.exp2(s * (SCALE * LOG2E) + (bias - lse))
    ds = (p * (dp - delta)).astype(BF16)
    p = p.astype(BF16)
    gv = jnp.dot(p, g, preferred_element_type=F32)
    gk = jnp.dot(ds, q, preferred_element_type=F32)
    gq = lax.dot_general(ds, k, (((0,), (0,)), ((), ())), preferred_element_type=F32)
    return gq, gk, gv


def local_kernel(at, own, recv, gq_out, gkv_out, kv_sums, q_late, *, ctx_count):
    kpos = positions(at[0], 0, ctx_count, False)
    qpos = positions(at[0], 1, ctx_count, False)
    bias = jnp.where(kpos <= qpos, 0.0, LOW)
    lse, delta = row_stats(own, recv)
    for kv in range(KV_OWN):
        k = jnp.concatenate([own[AT_K + kv], recv[AT_K + kv]], axis=0)
        v = jnp.concatenate([own[AT_V + kv], recv[AT_V + kv]], axis=0)
        gk = gv = None
        for j in range(GROUP):
            h = kv * GROUP + j
            q = jnp.concatenate([own[AT_Q + h], recv[AT_Q + h]], axis=0)
            g = jnp.concatenate([own[AT_G + h], recv[AT_G + h]], axis=0)
            tq, tk, tv = head_terms(q, g, k, v, bias, lse[h : h + 1], delta[h : h + 1])
            gq_out[h] = tq
            gk = tk if gk is None else gk + tk
            gv = tv if gv is None else gv + tv
        for row, t in ((kv, gk * SCALE), (KV_OWN + kv, gv)):
            gkv_out[row] = t
            kv_sums[row : row + 1, :] = jnp.sum(t, axis=0, keepdims=True)


    for h in range(GROUP):
        q_late[h, :HALF] = own[AT_Q + h, HALF:]
        q_late[h, HALF:] = recv[AT_Q + h, HALF:]
    q_late[GROUP, :HALF] = own[AT_ROW, :HALF]
    q_late[GROUP, HALF:] = recv[AT_ROW, :HALF]


def extra_kernel(at, own, recv, far, cross, q_late, out, *, ctx_count):
    k = jnp.concatenate([own[AT_K], recv[AT_K]], axis=0)
    v = jnp.concatenate([own[AT_V], recv[AT_V]], axis=0)
    lse, delta = (
        jnp.concatenate([a[:, HALF:], b[:, HALF:]], axis=1)
        for a, b in zip(
            pack_stats(q_late[GROUP, :HALF].astype(F32)), pack_stats(q_late[GROUP, HALF:].astype(F32))
        )
    )
    gk = gv = None
    for h in range(GROUP):
        g = jnp.concatenate([far[0, 1, h], cross[1, h]], axis=0)
        _, tk, tv = head_terms(q_late[h], g, k, v, 0.0, lse[h : h + 1], delta[h : h + 1])
        gk = tk if gk is None else gk + tk
        gv = tv if gv is None else gv + tv
    high_chip = at[0] >= ctx_count // 2
    out[0] = jnp.where(high_chip, gk * SCALE, 0.0)
    out[1] = jnp.where(high_chip, gv, 0.0)


def remote_kernel(
    at, own, recv, far, cross, gq_in, kv_sums, gq_same, gq_other, r, sums, *, ctx_count
):
    low_chip = at[0] < ctx_count // 2
    terms = []
    far_kv = (far.at[0, 0], cross.at[0], far.at[0, 1], cross.at[1])
    totals = []
    far_index = (at[0] + ctx_count // 2) % ctx_count
    kpos = positions(far_index, 0, ctx_count, True)
    qpos = positions(at[0], 1, ctx_count, False)
    bias = jnp.where(kpos <= qpos, 0.0, LOW)
    lse, delta = row_stats(own, recv)
    for kv in range(KV_OWN):
        k = jnp.concatenate([r[kv] for r in far_kv], axis=0)
        v = jnp.concatenate([r[KV_OWN + kv] for r in far_kv], axis=0)
        gk = gv = None
        for j in range(GROUP):
            h = kv * GROUP + j
            q = jnp.concatenate([own[AT_Q + h], recv[AT_Q + h]], axis=0)
            g = jnp.concatenate([own[AT_G + h], recv[AT_G + h]], axis=0)
            tq, tk, tv = head_terms(q, g, k, v, bias, lse[h : h + 1], delta[h : h + 1])
            gq = (gq_in[h] + tq) * SCALE
            gq_same[h] = gq[:ROWS].astype(BF16)
            gq_other[h] = gq[ROWS:].astype(BF16)
            totals.append((h, jnp.sum(gq, axis=0, keepdims=True)))
            gk = tk if gk is None else gk + tk
            gv = tv if gv is None else gv + tv
        for row, t in ((kv, gk * SCALE), (KV_OWN + kv, gv)):
            terms.append((row, t))
            total = jnp.sum(t, axis=0, keepdims=True) + kv_sums[row : row + 1, :]
            totals.append((Q_OWN + row, total))
    terms = [t for _, t in sorted(terms, key=lambda t: t[0])]
    for i in range(2 * KV_OWN):
        late = i % 2
        low = terms[KV_OWN * (i // 2) + 1][late * ROWS : (late + 1) * ROWS]
        r[i * ROWS : (i + 1) * ROWS, :] = jnp.where(low_chip, low, terms[i][:ROWS])
    pad = SUM_ROWS - len(totals)
    totals = [t for _, t in sorted(totals, key=lambda t: t[0])] + [jnp.zeros((pad, HEAD_SIZE), F32)]
    totals = jnp.concatenate(totals, axis=0)
    sums[...] = totals
    r[2 * KV_OWN * ROWS :, :] = totals


def cross_kernel(at, far, out):
    out[...] = far[1]


def kv_kernel(at, gkv, extra, r, gq_same, gq_other, sums, same, other, copies, *, ctx_count):
    low_chip = at[0] < ctx_count // 2
    both = sums[...] + r[2 * KV_OWN * ROWS :, :]
    copies[...] = jnp.broadcast_to(both[None], copies.shape)
    same[:Q_OWN] = gq_same[...]
    other[:Q_OWN] = gq_other[...]
    block_of = lambda i: r[i * ROWS : (i + 1) * ROWS, :]
    for i in range(2 * KV_OWN):
        for late in range(2):
            from_low = block_of(KV_OWN * (i // KV_OWN) + late) if i % KV_OWN else None
            from_high = block_of(i) if late == 0 else None
            zero = jnp.zeros((ROWS, HEAD_SIZE), F32)
            got = jnp.where(
                low_chip,
                zero if from_high is None else from_high,
                zero if from_low is None else from_low,
            )
            for out, block in ((same, 0), (other, 1)):
                rows = slice(block * ROWS + late * HALF, block * ROWS + (late + 1) * HALF)
                t = gkv[i, rows] + got[block * HALF : (block + 1) * HALF]
                if i % KV_OWN == 0:
                    t = t + extra[i // KV_OWN, rows]
                out[Q_OWN + i, late * HALF : (late + 1) * HALF] = t.astype(BF16)


def join_kernel(at, same, other, out_q, out_k, out_v):
    core = at[0] % 2
    for part, side in ((same, core), (other, 1 - core)):
        base = pl.multiple_of(side * (Q_OWN * HEAD_SIZE), Q_OWN * HEAD_SIZE)
        for h in range(Q_OWN):
            out_q[:, pl.ds(base + h * HEAD_SIZE, HEAD_SIZE)] = part[h]
        base = pl.multiple_of(side * (KV_OWN * HEAD_SIZE), KV_OWN * HEAD_SIZE)
        for h in range(KV_OWN):
            cols = pl.ds(base + h * HEAD_SIZE, HEAD_SIZE)
            out_k[:, cols] = part[Q_OWN + h]
            out_v[:, cols] = part[Q_OWN + KV_OWN + h]


def replica_sums_kernel(at, parts, out):
    total = parts[0]
    for r in range(1, parts.shape[0]):
        total = total + parts[r]
    out[...] = total


def join_sums_kernel(at, same, other, out_q, out_k, out_v):
    core = at[0] % 2
    for part, side in ((same, core), (other, 1 - core)):
        base = pl.multiple_of(side * (Q_OWN * HEAD_SIZE), Q_OWN * HEAD_SIZE)
        kv_base = pl.multiple_of(side * (KV_OWN * HEAD_SIZE), KV_OWN * HEAD_SIZE)
        for h in range(Q_OWN):
            out_q[:, pl.ds(base + h * HEAD_SIZE, HEAD_SIZE)] = part[h : h + 1, :]
        for h in range(KV_OWN):
            cols = pl.ds(kv_base + h * HEAD_SIZE, HEAD_SIZE)
            row = Q_OWN + h
            out_k[:, cols] = part[row : row + 1, :]
            row += KV_OWN
            out_v[:, cols] = part[row : row + 1, :]


def swapped(value, axis, bit):
    size = lax.axis_size(axis)
    return lax.ppermute(value, axis, [(i, i ^ bit) for i in range(size)])


def body(q_in, k_in, v_in, o_in, g_in, lse, bq, bk, bv):
    n = lax.axis_size("ctx")
    at = lax.axis_index("ctx").astype(jnp.int32).reshape(1)
    chips = n // 2
    blocks = lambda count, rows=ROWS, dtype=BF16: shape(count, rows, HEAD_SIZE, dtype=dtype)

    dp = lax.axis_size("dp")
    own, send, kvz = call(
        functools.partial(prep_kernel, ctx_count=n),
        [blocks(PACK), blocks(PACK), shape(2, 2, 2 * KV_OWN, HALF, HEAD_SIZE)],
        9,
        moved=4 << 20,
        vmem=60 << 20,
    )(at, q_in[0, 0], k_in[0, 0], v_in[0, 0], o_in[0, 0], g_in[0, 0], lse[0, 0], bq, bk, bv)

    far = held(swapped(kvz, "ctx", chips))
    recv = held(swapped(send, "ctx", 1))
    own = held(own)

    gq, gkv, kv_sums, q_late = call(
        functools.partial(local_kernel, ctx_count=n),
        [blocks(Q_OWN, 2 * ROWS, F32), blocks(2 * KV_OWN, 2 * ROWS, F32)]
        + [shape(2 * KV_OWN, HEAD_SIZE, dtype=F32), blocks(GROUP + 1)],
        2,
        flops=700_000_000,
        moved=3 << 20,
    )(at, own, recv)
    q_late = held(lax.ppermute(q_late, "ctx", [(i, i + chips) for i in range(chips)]))

    def before(x, bit):
        pairs = []
        for s in range(1, lax.axis_size("section")):
            pairs += [(s * n + c, (s - 1) * n + (c ^ bit)) for c in range(n)]
        return held(lax.ppermute(x, ("section", "ctx"), pairs))

    (cross,) = call(cross_kernel, [shape(2, 2 * KV_OWN, HALF, HEAD_SIZE)], 1)(at, far)
    cross = held(swapped(cross, "ctx", 1))
    gq_same, gq_other, r, sums = call(
        functools.partial(remote_kernel, ctx_count=n),
        [blocks(Q_OWN)] * 2
        + [
            shape(2 * KV_OWN * ROWS + SUM_ROWS, HEAD_SIZE, dtype=F32),
            shape(SUM_ROWS, HEAD_SIZE, dtype=F32),
        ],
        6,
        flops=700_000_000,
        moved=4 << 20,
    )(at, own, recv, far, cross, held(gq), held(kv_sums))

    r = held(swapped(r, "ctx", chips))
    (extra,) = call(
        functools.partial(extra_kernel, ctx_count=n),
        [blocks(2, 2 * ROWS, F32)],
        5,
        flops=150_000_000,
        moved=1 << 20,
    )(at, own, recv, far, cross, q_late)
    same, other, copies = call(
        functools.partial(kv_kernel, ctx_count=n),
        [blocks(Q_OWN + 2 * KV_OWN)] * 2 + [shape(dp, SUM_ROWS, HEAD_SIZE, dtype=F32)],
        6,
        moved=2 << 20,
        keep=2,
    )(at, held(gkv), held(extra), r, held(gq_same), held(gq_other), held(sums))
    same, other = before(same, 0), before(other, 1)
    copies = held(lax.all_to_all(copies, "dp", 0, 0, tiled=True))
    (sums,) = call(replica_sums_kernel, [shape(SUM_ROWS, HEAD_SIZE, dtype=F32)], 1)(at, copies)
    sum_q, sum_k, sum_v = call(
        join_sums_kernel,
        [
            shape(1, Q_HEADS * HEAD_SIZE, dtype=F32),
            shape(1, KV_HEADS * HEAD_SIZE, dtype=F32),
            shape(1, KV_HEADS * HEAD_SIZE, dtype=F32),
        ],
        2,
        keep=False,
    )(at, held(sums), held(swapped(sums, "ctx", 1)))
    recv_q, recv_k, recv_v = call(
        join_kernel,
        [shape(ROWS, Q_HEADS * HEAD_SIZE)] + [shape(ROWS, KV_HEADS * HEAD_SIZE)] * 2,
        2,
        moved=3 << 19,
        keep=False,
    )(at, same, other)
    return (recv_q[None, None], recv_k[None, None], recv_v[None, None], sum_q, sum_k, sum_v)


def solution(mesh):
    return jax.shard_map(
        body,
        mesh=mesh,
        in_specs=(
            P("dp", "section", "ctx", None),
            P("dp", "section", "ctx", None),
            P("dp", "section", "ctx", None),
            P("dp", "section", "ctx", None),
            P("dp", "section", "ctx", None),
            P("dp", "section", None, "ctx"),
            P("section", None),
            P("section", None),
            P("section", None),
        ),
        out_specs=(
            P("dp", "section", "ctx", None),
            P("dp", "section", "ctx", None),
            P("dp", "section", "ctx", None),
            P("section", None),
            P("section", None),
            P("section", None),
        ),
        check_vma=False,
    )
```

```python
import functools
import math

import jax
import jax.numpy as jnp
from jax import lax
from jax.experimental import pallas as pl
from jax.experimental.pallas import tpu as pltpu
from jax.sharding import PartitionSpec as P


HEAD_SIZE = 128
ROWS = 128
HALF = ROWS // 2
Q_HEADS = 16
KV_HEADS = 4
Q_OWN = Q_HEADS // 2
KV_OWN = KV_HEADS // 2
GROUP = Q_HEADS // KV_HEADS
SCALE = 1.0 / math.sqrt(HEAD_SIZE)
LOG2E = math.log2(math.e)
AT_Q = 0
AT_G = AT_Q + Q_OWN
AT_K = AT_G + Q_OWN
AT_V = AT_K + KV_OWN
AT_ROW = AT_V + KV_OWN
PACK = AT_ROW + 1
SUM_ROWS = 16
BF16 = jnp.bfloat16
F32 = jnp.float32
LOW = -1e30
KERNEL_VMEM = 24 << 20

SMEM = pl.BlockSpec(memory_space=pltpu.SMEM)
VMEM = pl.BlockSpec(memory_space=pltpu.VMEM)


def call(kernel, outs, n_in, flops=0, moved=0, keep=True, vmem=KERNEL_VMEM):
    keep = len(outs) if keep is True else int(keep)
    outs = [pltpu.VMEM(o.shape, o.dtype) for o in outs[:keep]] + outs[keep:]
    run = pl.pallas_call(
        kernel,
        out_shape=outs,
        in_specs=[SMEM] + [VMEM] * n_in,
        out_specs=[VMEM] * len(outs),
        compiler_params=pltpu.CompilerParams(vmem_limit_bytes=vmem),
        cost_estimate=pl.CostEstimate(flops=flops, bytes_accessed=moved, transcendentals=0),
    )
    return run


def held(x):
    return pltpu.with_memory_space_constraint(x, pltpu.VMEM)


def shape(*dims, dtype=BF16):
    return jax.ShapeDtypeStruct(dims, dtype)


def split3(x):
    a = x.astype(BF16)
    rest = x - a.astype(F32)
    b = rest.astype(BF16)
    return a, b, (rest - b.astype(F32)).astype(BF16)


def prep_kernel(at, q, k, v, o, g, lse, bq, bk, bv, own, send, kvz, *, ctx_count):
    core = at[0] % 2
    low_chip = at[0] < ctx_count // 2
    for pack, side in ((own, core), (send, 1 - core)):
        base = pl.multiple_of(side * (Q_OWN * HEAD_SIZE), Q_OWN * HEAD_SIZE)
        kv_base = pl.multiple_of(side * (KV_OWN * HEAD_SIZE), KV_OWN * HEAD_SIZE)
        deltas = []
        for h in range(Q_OWN):
            cols = pl.ds(base + h * HEAD_SIZE, HEAD_SIZE)
            pack[AT_Q + h] = (q[:, cols].astype(F32) + bq[:, cols].astype(F32)).astype(BF16)
            grad = g[:, cols]
            pack[AT_G + h] = grad
            deltas.append(
                jnp.sum(grad.astype(F32) * o[:, cols].astype(F32), axis=1, keepdims=True)
            )
        to = 0 if pack is own else 1
        for h in range(KV_OWN):
            cols = pl.ds(kv_base + h * HEAD_SIZE, HEAD_SIZE)
            kb = (k[:, cols].astype(F32) + bk[:, cols].astype(F32)).astype(BF16)
            vb = (v[:, cols].astype(F32) + bv[:, cols].astype(F32)).astype(BF16)
            pack[AT_K + h] = kb
            pack[AT_V + h] = vb
            for i, t in ((h, kb), (KV_OWN + h, vb)):
                kvz[to, 0, i] = t[:HALF]
                kvz[to, 1, i] = jnp.where(low_chip, pack[AT_G + i, HALF:], t[HALF:])
        delta = jnp.concatenate(deltas + [jnp.zeros((ROWS, HEAD_SIZE - Q_OWN), F32)], axis=1).T
        heads = pl.ds(pl.multiple_of(side * Q_OWN, Q_OWN), Q_OWN)
        stats = jnp.concatenate(
            [p.astype(F32) for p in split3(lse[heads, :])]
            + [p.astype(F32) for p in split3(delta[:Q_OWN])]
            + [jnp.zeros((ROWS - 6 * Q_OWN, HEAD_SIZE), F32)],
            axis=0,
        )
        pack[AT_ROW] = stats.astype(BF16)


def pack_stats(s):
    n = Q_OWN
    lse = (s[:n] + s[n : 2 * n]) + s[2 * n : 3 * n]
    delta = (s[3 * n : 4 * n] + s[4 * n : 5 * n]) + s[5 * n : 6 * n]
    return lse * LOG2E, delta


def row_stats(own, recv):
    (la, da), (lb, db) = (pack_stats(p[AT_ROW].astype(F32)) for p in (own, recv))
    return jnp.concatenate([la, lb], axis=1), jnp.concatenate([da, db], axis=1)


def positions(index, dim, ctx_count, alternate):
    i = lax.broadcasted_iota(jnp.int32, (2 * ROWS, 2 * ROWS), dim)
    part = i // HALF
    late = part // 2 if alternate else part % 2
    other = part % 2 if alternate else part // 2
    block = jnp.where(other == 1, index + 1 - 2 * (index % 2), index)
    half = jnp.where(late == 1, 2 * ctx_count - 1 - block, block)
    return half * HALF + i % HALF


def head_terms(q, g, k, v, bias, lse, delta):
    s = lax.dot_general(k, q, (((1,), (1,)), ((), ())), preferred_element_type=F32)
    dp = lax.dot_general(v, g, (((1,), (1,)), ((), ())), preferred_element_type=F32)
    p = jnp.exp2(s * (SCALE * LOG2E) + (bias - lse))
    ds = (p * (dp - delta)).astype(BF16)
    p = p.astype(BF16)
    gv = jnp.dot(p, g, preferred_element_type=F32)
    gk = jnp.dot(ds, q, preferred_element_type=F32)
    gq = lax.dot_general(ds, k, (((0,), (0,)), ((), ())), preferred_element_type=F32)
    return gq, gk, gv


def local_kernel(at, own, recv, gq_out, gkv_out, kv_sums, q_late, *, ctx_count):
    kpos = positions(at[0], 0, ctx_count, False)
    qpos = positions(at[0], 1, ctx_count, False)
    bias = jnp.where(kpos <= qpos, 0.0, LOW)
    lse, delta = row_stats(own, recv)
    for kv in range(KV_OWN):
        k = jnp.concatenate([own[AT_K + kv], recv[AT_K + kv]], axis=0)
        v = jnp.concatenate([own[AT_V + kv], recv[AT_V + kv]], axis=0)
        gk = gv = None
        for j in range(GROUP):
            h = kv * GROUP + j
            q = jnp.concatenate([own[AT_Q + h], recv[AT_Q + h]], axis=0)
            g = jnp.concatenate([own[AT_G + h], recv[AT_G + h]], axis=0)
            tq, tk, tv = head_terms(q, g, k, v, bias, lse[h : h + 1], delta[h : h + 1])
            gq_out[h] = tq
            gk = tk if gk is None else gk + tk
            gv = tv if gv is None else gv + tv
        for row, t in ((kv, gk * SCALE), (KV_OWN + kv, gv)):
            gkv_out[row] = t
            kv_sums[row : row + 1, :] = jnp.sum(t, axis=0, keepdims=True)


    for h in range(GROUP):
        q_late[h, :HALF] = own[AT_Q + h, HALF:]
        q_late[h, HALF:] = recv[AT_Q + h, HALF:]
    q_late[GROUP, :HALF] = own[AT_ROW, :HALF]
    q_late[GROUP, HALF:] = recv[AT_ROW, :HALF]


def extra_kernel(at, own, recv, far, cross, q_late, out, *, ctx_count):
    k = jnp.concatenate([own[AT_K], recv[AT_K]], axis=0)
    v = jnp.concatenate([own[AT_V], recv[AT_V]], axis=0)
    lse, delta = (
        jnp.concatenate([a[:, HALF:], b[:, HALF:]], axis=1)
        for a, b in zip(
            pack_stats(q_late[GROUP, :HALF].astype(F32)), pack_stats(q_late[GROUP, HALF:].astype(F32))
        )
    )
    gk = gv = None
    for h in range(GROUP):
        g = jnp.concatenate([far[0, 1, h], cross[1, h]], axis=0)
        _, tk, tv = head_terms(q_late[h], g, k, v, 0.0, lse[h : h + 1], delta[h : h + 1])
        gk = tk if gk is None else gk + tk
        gv = tv if gv is None else gv + tv
    high_chip = at[0] >= ctx_count // 2
    out[0] = jnp.where(high_chip, gk * SCALE, 0.0)
    out[1] = jnp.where(high_chip, gv, 0.0)


def remote_kernel(
    at, own, recv, far, cross, gq_in, kv_sums, gq_same, gq_other, r, sums, *, ctx_count
):
    low_chip = at[0] < ctx_count // 2
    terms = []
    far_kv = (far.at[0, 0], cross.at[0], far.at[0, 1], cross.at[1])
    totals = []
    far_index = (at[0] + ctx_count // 2) % ctx_count
    kpos = positions(far_index, 0, ctx_count, True)
    qpos = positions(at[0], 1, ctx_count, False)
    bias = jnp.where(kpos <= qpos, 0.0, LOW)
    lse, delta = row_stats(own, recv)
    for kv in range(KV_OWN):
        k = jnp.concatenate([r[kv] for r in far_kv], axis=0)
        v = jnp.concatenate([r[KV_OWN + kv] for r in far_kv], axis=0)
        gk = gv = None
        for j in range(GROUP):
            h = kv * GROUP + j
            q = jnp.concatenate([own[AT_Q + h], recv[AT_Q + h]], axis=0)
            g = jnp.concatenate([own[AT_G + h], recv[AT_G + h]], axis=0)
            tq, tk, tv = head_terms(q, g, k, v, bias, lse[h : h + 1], delta[h : h + 1])
            gq = (gq_in[h] + tq) * SCALE
            gq_same[h] = gq[:ROWS].astype(BF16)
            gq_other[h] = gq[ROWS:].astype(BF16)
            totals.append((h, jnp.sum(gq, axis=0, keepdims=True)))
            gk = tk if gk is None else gk + tk
            gv = tv if gv is None else gv + tv
        for row, t in ((kv, gk * SCALE), (KV_OWN + kv, gv)):
            terms.append((row, t))
            total = jnp.sum(t, axis=0, keepdims=True) + kv_sums[row : row + 1, :]
            totals.append((Q_OWN + row, total))
    terms = [t for _, t in sorted(terms, key=lambda t: t[0])]
    for i in range(2 * KV_OWN):
        late = i % 2
        low = terms[KV_OWN * (i // 2) + 1][late * ROWS : (late + 1) * ROWS]
        r[i * ROWS : (i + 1) * ROWS, :] = jnp.where(low_chip, low, terms[i][:ROWS])
    pad = SUM_ROWS - len(totals)
    totals = [t for _, t in sorted(totals, key=lambda t: t[0])] + [jnp.zeros((pad, HEAD_SIZE), F32)]
    sums[...] = jnp.broadcast_to(jnp.concatenate(totals, axis=0)[None], sums.shape)


def cross_kernel(at, far, out):
    out[...] = far[1]


def kv_kernel(at, gkv, extra, r, gq_same, gq_other, same, other, *, ctx_count):
    low_chip = at[0] < ctx_count // 2
    same[:Q_OWN] = gq_same[...]
    other[:Q_OWN] = gq_other[...]
    block_of = lambda i: r[i * ROWS : (i + 1) * ROWS, :]
    for i in range(2 * KV_OWN):
        for late in range(2):
            from_low = block_of(KV_OWN * (i // KV_OWN) + late) if i % KV_OWN else None
            from_high = block_of(i) if late == 0 else None
            zero = jnp.zeros((ROWS, HEAD_SIZE), F32)
            got = jnp.where(
                low_chip,
                zero if from_high is None else from_high,
                zero if from_low is None else from_low,
            )
            for out, block in ((same, 0), (other, 1)):
                rows = slice(block * ROWS + late * HALF, block * ROWS + (late + 1) * HALF)
                t = gkv[i, rows] + got[block * HALF : (block + 1) * HALF]
                if i % KV_OWN == 0:
                    t = t + extra[i // KV_OWN, rows]
                out[Q_OWN + i, late * HALF : (late + 1) * HALF] = t.astype(BF16)


def join_kernel(at, same, other, out_q, out_k, out_v):
    core = at[0] % 2
    for part, side in ((same, core), (other, 1 - core)):
        base = pl.multiple_of(side * (Q_OWN * HEAD_SIZE), Q_OWN * HEAD_SIZE)
        for h in range(Q_OWN):
            out_q[:, pl.ds(base + h * HEAD_SIZE, HEAD_SIZE)] = part[h]
        base = pl.multiple_of(side * (KV_OWN * HEAD_SIZE), KV_OWN * HEAD_SIZE)
        for h in range(KV_OWN):
            cols = pl.ds(base + h * HEAD_SIZE, HEAD_SIZE)
            out_k[:, cols] = part[Q_OWN + h]
            out_v[:, cols] = part[Q_OWN + KV_OWN + h]


def replica_sums_kernel(at, parts, out):
    total = parts[0]
    for r in range(1, parts.shape[0]):
        total = total + parts[r]
    out[...] = total


def stack_kernel(at, same, other, out):
    out[0] = same[...]
    out[1] = other[...]


def join_sums_kernel(at, chip, far, out_q, out_k, out_v):
    core = at[0] % 2
    for i, side in ((0, core), (1, 1 - core)):
        part = chip[i] + far[i]
        base = pl.multiple_of(side * (Q_OWN * HEAD_SIZE), Q_OWN * HEAD_SIZE)
        kv_base = pl.multiple_of(side * (KV_OWN * HEAD_SIZE), KV_OWN * HEAD_SIZE)
        for h in range(Q_OWN):
            out_q[:, pl.ds(base + h * HEAD_SIZE, HEAD_SIZE)] = part[h : h + 1, :]
        for h in range(KV_OWN):
            cols = pl.ds(kv_base + h * HEAD_SIZE, HEAD_SIZE)
            row = Q_OWN + h
            out_k[:, cols] = part[row : row + 1, :]
            row += KV_OWN
            out_v[:, cols] = part[row : row + 1, :]


def swapped(value, axis, bit):
    size = lax.axis_size(axis)
    return lax.ppermute(value, axis, [(i, i ^ bit) for i in range(size)])


def body(q_in, k_in, v_in, o_in, g_in, lse, bq, bk, bv):
    n = lax.axis_size("ctx")
    at = lax.axis_index("ctx").astype(jnp.int32).reshape(1)
    chips = n // 2
    blocks = lambda count, rows=ROWS, dtype=BF16: shape(count, rows, HEAD_SIZE, dtype=dtype)

    dp = lax.axis_size("dp")
    own, send, kvz = call(
        functools.partial(prep_kernel, ctx_count=n),
        [blocks(PACK), blocks(PACK), shape(2, 2, 2 * KV_OWN, HALF, HEAD_SIZE)],
        9,
        moved=4 << 20,
        vmem=60 << 20,
    )(at, q_in[0, 0], k_in[0, 0], v_in[0, 0], o_in[0, 0], g_in[0, 0], lse[0, 0], bq, bk, bv)

    far = held(swapped(kvz, "ctx", chips))
    recv = held(swapped(send, "ctx", 1))
    own = held(own)

    gq, gkv, kv_sums, q_late = call(
        functools.partial(local_kernel, ctx_count=n),
        [blocks(Q_OWN, 2 * ROWS, F32), blocks(2 * KV_OWN, 2 * ROWS, F32)]
        + [shape(2 * KV_OWN, HEAD_SIZE, dtype=F32), blocks(GROUP + 1)],
        2,
        flops=700_000_000,
        moved=3 << 20,
    )(at, own, recv)
    q_late = held(lax.ppermute(q_late, "ctx", [(i, i + chips) for i in range(chips)]))

    def before(x, bit):
        pairs = []
        for s in range(1, lax.axis_size("section")):
            pairs += [(s * n + c, (s - 1) * n + (c ^ bit)) for c in range(n)]
        return held(lax.ppermute(x, ("section", "ctx"), pairs))

    (cross,) = call(cross_kernel, [shape(2, 2 * KV_OWN, HALF, HEAD_SIZE)], 1)(at, far)
    cross = held(swapped(cross, "ctx", 1))
    gq_same, gq_other, r, sums = call(
        functools.partial(remote_kernel, ctx_count=n),
        [blocks(Q_OWN)] * 2
        + [
            shape(2 * KV_OWN * ROWS, HEAD_SIZE, dtype=F32),
            shape(dp, SUM_ROWS, HEAD_SIZE, dtype=F32),
        ],
        6,
        flops=700_000_000,
        moved=4 << 20,
        keep=3,
    )(at, own, recv, far, cross, held(gq), held(kv_sums))
    parts = held(lax.all_to_all(sums, "dp", 0, 0, tiled=True))

    r = held(swapped(r, "ctx", chips))
    (extra,) = call(
        functools.partial(extra_kernel, ctx_count=n),
        [blocks(2, 2 * ROWS, F32)],
        5,
        flops=150_000_000,
        moved=1 << 20,
    )(at, own, recv, far, cross, q_late)
    same, other = call(
        functools.partial(kv_kernel, ctx_count=n),
        [blocks(Q_OWN + 2 * KV_OWN)] * 2,
        5,
        moved=2 << 20,
    )(at, held(gkv), held(extra), r, held(gq_same), held(gq_other))
    same, other = before(same, 0), before(other, 1)
    (sums,) = call(replica_sums_kernel, [shape(SUM_ROWS, HEAD_SIZE, dtype=F32)], 1)(at, parts)
    sums_other = swapped(sums, "ctx", 1)
    (chip_sums,) = call(
        stack_kernel, [shape(2, SUM_ROWS, HEAD_SIZE, dtype=F32)], 2
    )(at, held(sums), held(sums_other))
    far_sums = swapped(chip_sums, "ctx", chips)
    sum_q, sum_k, sum_v = call(
        join_sums_kernel,
        [
            shape(1, Q_HEADS * HEAD_SIZE, dtype=F32),
            shape(1, KV_HEADS * HEAD_SIZE, dtype=F32),
            shape(1, KV_HEADS * HEAD_SIZE, dtype=F32),
        ],
        2,
        keep=False,
    )(at, held(chip_sums), held(far_sums))
    recv_q, recv_k, recv_v = call(
        join_kernel,
        [shape(ROWS, Q_HEADS * HEAD_SIZE)] + [shape(ROWS, KV_HEADS * HEAD_SIZE)] * 2,
        2,
        moved=3 << 19,
        keep=False,
    )(at, same, other)
    return (recv_q[None, None], recv_k[None, None], recv_v[None, None], sum_q, sum_k, sum_v)


def solution(mesh):
    return jax.shard_map(
        body,
        mesh=mesh,
        in_specs=(
            P("dp", "section", "ctx", None),
            P("dp", "section", "ctx", None),
            P("dp", "section", "ctx", None),
            P("dp", "section", "ctx", None),
            P("dp", "section", "ctx", None),
            P("dp", "section", None, "ctx"),
            P("section", None),
            P("section", None),
            P("section", None),
        ),
        out_specs=(
            P("dp", "section", "ctx", None),
            P("dp", "section", "ctx", None),
            P("dp", "section", "ctx", None),
            P("section", None),
            P("section", None),
            P("section", None),
        ),
        check_vma=False,
    )
```
